256 devices in a mesh: rel: 4 (over y), ent: 64 (over x, z, core).
Axes of the slice: x: 4, y: 4, z: 8, core: 2. Of those that a mesh axis runs over, the one named last changes fastest.
Arguments:
- factor: bfloat16 [16384, 512], P('ent'), may hold values from -1 to 1
- core_tensors: bfloat16 [32, 512, 512], P('rel'), may hold values from -0.25 to 0.25
- tile_values: bfloat16 [4, 4608, 128, 128], P('rel', 'ent'), may hold values from -4096 to 4096
- tile_rel: int32 [4, 4608], P('rel', 'ent'), may hold values from 0 to 7
- tile_block: int32 [4, 4608], P('rel', 'ent'), may hold values from 0 to 1
- tile_col: int32 [4, 4608], P('rel', 'ent'), may hold values from 0 to 127, as said below
- tile_flip: int32 [4, 4608], P('rel', 'ent'), may hold values from 0 to 1
- tile_count: int32 [4, 64], P('rel', 'ent'), may hold values from 64 to 72, as said below
Outputs:
- updated: float32 [16384, 512], P('ent')
The draws below stay inside these ranges and needn't reach their ends.
Inputs may be any that keep to these rules, and one draw needn't show every extreme that they name: `tile_count`: live slots per device; the first 64 slots of every device are live, and in every group one device has all 72 slots live. `tile_col`: all slots of one device whose column blocks lie on one index of ent (column block // 2) name the same column block; the first 64 slots of a device name every index of ent once.
All inputs are finite; a program needn't handle non-finite values.
Results may differ from the reference program's by a relative error of at most 0.0036.
Values may be sent and summed in bfloat16 or wider, within the bound.
No kernel may reach another device: no remote copies, remote signals or barrier semaphores. Data moves between devices by JAX's collectives and lax.ppermute only.
A program may use at most 128 MiB of HBM per device.

```python
import math
import jax
import jax.numpy as jnp
from jax import lax

RANK = 512
REL_GROUP = 8
TILE = 128
BLOCKS_DEV = 2
GROUPS = 4
TILES_DEV = 72
RELS = 32
ENTITIES = 16384
SLOTS = 4608
N_ENT = 64


def layout(key):
    devices = SLOTS // TILES_DEV
    extra = TILES_DEV - devices
    subkeys = jax.random.split(jax.random.fold_in(key, 7), 8)
    relation_ids = jax.random.randint(subkeys[0], (GROUPS, SLOTS), 0, REL_GROUP)
    block_ids = jax.random.randint(subkeys[1], (GROUPS, SLOTS), 0, BLOCKS_DEV)
    random_owners = jax.random.randint(subkeys[2], (GROUPS, SLOTS), 0, devices)
    scores = jax.random.randint(subkeys[7], (GROUPS, devices, devices), 0, 1 << 20)
    scores = scores * devices + jnp.arange(devices, dtype=jnp.int32)[None, None, :]
    orders = jnp.argsort(scores, axis=2).astype(jnp.int32)
    reader = jnp.arange(SLOTS, dtype=jnp.int32) // TILES_DEV
    local = jnp.arange(SLOTS, dtype=jnp.int32) % TILES_DEV
    group_ids = jnp.arange(GROUPS, dtype=jnp.int32)
    first_owners = orders[group_ids[:, None], reader[None, :], jnp.minimum(local, devices - 1)[None, :]]
    owners = jnp.where((local < devices)[None, :], first_owners, random_owners)
    picked = jax.random.randint(subkeys[3], (GROUPS, devices, devices), 0, BLOCKS_DEV)
    picked = picked.at[0, 0, devices - 1].set(BLOCKS_DEV - 1)
    inner_block = picked[group_ids[:, None], reader[None, :], owners]
    columns = owners * BLOCKS_DEV + inner_block
    flip_bits = jax.random.randint(subkeys[4], (GROUPS, SLOTS), 0, 2)
    levels = jax.random.randint(subkeys[5], (GROUPS, devices), 0, extra)
    counts = devices + levels * levels // extra
    busiest = jax.random.randint(subkeys[6], (GROUPS, 1), 0, devices)
    counts = jnp.where(jnp.arange(devices, dtype=jnp.int32)[None, :] == busiest, TILES_DEV, counts)
    return (relation_ids, block_ids, columns, flip_bits, counts)


def draw_tile_rel(key, part):
    return layout(key)[0].astype(jnp.int32)


def draw_tile_block(key, part):
    return layout(key)[1].astype(jnp.int32)


def draw_tile_col(key, part):
    return layout(key)[2].astype(jnp.int32)


def draw_tile_flip(key, part):
    return layout(key)[3].astype(jnp.int32)


def draw_tile_count(key, part):
    return layout(key)[4].astype(jnp.int32)


def draw_factor(key, part):
    subkeys = jax.random.split(jax.random.fold_in(key, 3), 2)
    column_scale = 0.3 * jnp.exp(jax.random.uniform(subkeys[1], (1, RANK), jnp.float32, 0.0, 1.0) * math.log(10.0))
    row_position = jnp.arange(ENTITIES, dtype=jnp.float32) / (ENTITIES - 1)
    entries = jax.random.normal(subkeys[0], (ENTITIES, RANK), jnp.float32)
    row_ramp = 1.0 + 2.0 * row_position
    entries = entries * column_scale * row_ramp[:, None] / math.sqrt(ENTITIES)
    return jnp.clip(entries, -1.0, 1.0).astype(jnp.bfloat16)


def steps_of(stream_key, extent, shards, low, high):
    level = 1.0
    for dim, shards_of in shards:
        draws = jax.random.uniform(jax.random.fold_in(jax.random.fold_in(stream_key, 6), dim), (shards_of,), jnp.float32, low / len(shards), high / len(shards))
        level = level * jnp.repeat(jnp.exp(draws), extent[dim] // shards_of).reshape((-1,) + (1,) * (len(extent) - 1 - dim))
    return level


def normal_values(rng, extent, width, reach, cuts=(), kind=jnp.bfloat16):
    array = width * jax.random.normal(rng, extent, jnp.float32)
    if cuts:
        array = array * steps_of(rng, extent, cuts, -0.22, 0.18)
    return jnp.clip(array, -reach, reach).astype(kind)


def setup_inputs(seed: int = 0) -> dict:
    key_of = jax.random.split(jax.random.key(seed), 9)
    return {
        "factor": draw_factor(jax.random.fold_in(key_of[8], 71), 0),
        "core_tensors": normal_values(key_of[1], (RELS, RANK, RANK), RANK ** -0.5, 0.25, ((0, 4),)),
        "tile_values": normal_values(key_of[2], (GROUPS, SLOTS, TILE, TILE), (64 * (ENTITIES / TILE) ** 0.5), 4096.0, ((0, 4), (1, 64))),
        "tile_rel": draw_tile_rel(jax.random.fold_in(key_of[8], 71), 0),
        "tile_block": draw_tile_block(jax.random.fold_in(key_of[8], 71), 0),
        "tile_col": draw_tile_col(jax.random.fold_in(key_of[8], 71), 0),
        "tile_flip": draw_tile_flip(jax.random.fold_in(key_of[8], 71), 0),
        "tile_count": draw_tile_count(jax.random.fold_in(key_of[8], 71), 0),
    }


ridge_weight = 16.0
top_precision = lax.Precision.HIGHEST

def reference(factor, core_tensors, tile_values, tile_rel, tile_block, tile_col, tile_flip, tile_count):
    factor_blocks = factor.astype(jnp.float32).reshape(ENTITIES // TILE, TILE, RANK)
    slot_ids = jnp.arange(TILES_DEV, dtype=jnp.int32)
    target_ids = jnp.arange(BLOCKS_DEV * 2 * REL_GROUP, dtype=jnp.int32)

    def device_rows(device):
        totals = jnp.zeros((BLOCKS_DEV * TILE, RANK), jnp.float32)
        first_slot = (device * TILES_DEV).astype(jnp.int32)
        for group_index in range(GROUPS):
            values = lax.dynamic_slice_in_dim(tile_values[group_index], first_slot, TILES_DEV, 0).astype(jnp.float32)
            relation_ids = lax.dynamic_slice_in_dim(tile_rel[group_index], first_slot, TILES_DEV, 0)
            block_ids = lax.dynamic_slice_in_dim(tile_block[group_index], first_slot, TILES_DEV, 0)
            columns = lax.dynamic_slice_in_dim(tile_col[group_index], first_slot, TILES_DEV, 0)
            flip_bits = lax.dynamic_slice_in_dim(tile_flip[group_index], first_slot, TILES_DEV, 0)
            live_slot = slot_ids < tile_count[group_index, device]
            factor_panels = jnp.take(factor_blocks, columns.astype(jnp.int32), axis=0)
            direction_aligned = jnp.where((flip_bits == 1)[:, None, None], jnp.swapaxes(values, 1, 2), values)
            tile_contributions = jnp.einsum('ujl,uld->ujd', direction_aligned, factor_panels, precision=top_precision)
            targets = (block_ids * 2 + flip_bits) * REL_GROUP + relation_ids
            indicator_matrix = ((targets[None, :] == target_ids[:, None]) & live_slot[None, :]).astype(jnp.float32)
            indicator_matrix = indicator_matrix.reshape(BLOCKS_DEV, 2, REL_GROUP, TILES_DEV)
            block_totals_sum = jnp.einsum('byvr,rex->beyvx', indicator_matrix, tile_contributions, precision=top_precision).astype(jnp.bfloat16)
            group_cores = core_tensors[group_index * REL_GROUP:(group_index + 1) * REL_GROUP]
            weights = jnp.concatenate([jnp.swapaxes(group_cores, 1, 2), group_cores], axis=0)
            weights = weights.reshape(2 * REL_GROUP * RANK, RANK).astype(jnp.float32)
            flat_sums = block_totals_sum.astype(jnp.float32).reshape(BLOCKS_DEV * TILE, 2 * REL_GROUP * RANK)
            totals = totals + jnp.dot(flat_sums, weights, precision=top_precision)
        return totals
    rows_sum = lax.map(device_rows, jnp.arange(N_ENT, dtype=jnp.int32)).reshape(ENTITIES, RANK)
    factor_wide = factor.astype(jnp.float32)
    gram_matrix = jnp.dot(factor_wide.T, factor_wide, precision=top_precision)

    def add_relation(running, core_matrix):
        core_matrix = core_matrix.astype(jnp.float32)
        left_term = jnp.dot(jnp.dot(core_matrix, gram_matrix, precision=top_precision), core_matrix.T, precision=top_precision)
        right_term = jnp.dot(jnp.dot(core_matrix.T, gram_matrix, precision=top_precision), core_matrix, precision=top_precision)
        return (running + left_term + right_term, None)
    system, unused = lax.scan(add_relation, ridge_weight * jnp.eye(RANK, dtype=jnp.float32), core_tensors)
    lower_factor = jnp.linalg.cholesky(system)
    return jax.scipy.linalg.cho_solve((lower_factor, True), rows_sum.T).T
```

```python
import jax
import jax.numpy as jnp
from jax import lax
from jax.experimental import pallas as pl
from jax.experimental.pallas import tpu as pltpu
from jax.sharding import PartitionSpec as P

HI = lax.Precision.HIGHEST
VM = 60 * 1024 * 1024

def dg(a, b, ca, cb):
    return lax.dot_general(a, b, (((ca,), (cb,)), ((), ())), preferred_element_type=jnp.float32)

def system_kernel(a_ref, core_ref, out_ref, d0_ref, d1_ref, low_ref, c0_ref, c1_ref):
    rows = a_ref[...]
    sums = (d0_ref, d1_ref, low_ref, c0_ref, c1_ref)
    for ref in sums:
        ref[...] = jnp.zeros_like(ref)

    def body(step, carry):
        core = core_ref[step]
        term = jnp.concatenate([dg(rows, core, 1, 1), dg(rows, core, 1, 0)], axis=0)
        high = term.astype(jnp.bfloat16)
        low = (term - high.astype(jnp.float32)).astype(jnp.bfloat16)
        h0, h1 = high[:, :256], high[:, 256:]
        l0, l1 = low[:, :256], low[:, 256:]
        h0t, h1t, l1t = h0.T, h1.T, l1.T
        d0_ref[...] += jnp.dot(h0t, h0, preferred_element_type=jnp.float32)
        d1_ref[...] += jnp.dot(h1t, h1, preferred_element_type=jnp.float32)
        c0_ref[...] += jnp.dot(h0t, l0, preferred_element_type=jnp.float32)
        c1_ref[...] += jnp.dot(h1t, l1, preferred_element_type=jnp.float32)
        low_ref[...] += (
            jnp.dot(h1t, h0, preferred_element_type=jnp.float32)
            + jnp.dot(h1t, l0, preferred_element_type=jnp.float32)
            + jnp.dot(l1t, h0, preferred_element_type=jnp.float32)
        )
        return carry

    lax.fori_loop(0, core_ref.shape[0], body, 0)
    first = d0_ref[...] + (c0_ref[...] + c0_ref[...].T)
    last = d1_ref[...] + (c1_ref[...] + c1_ref[...].T)
    mixed = low_ref[...]
    parts = (
        first[:128, :128], first[128:, :128], first[128:, 128:],
        mixed[:128, :128], mixed[:128, 128:], last[:128, :128],
        mixed[128:, :128], mixed[128:, 128:], last[128:, :128], last[128:, 128:],
    )
    for index, part in enumerate(parts):
        out_ref[pl.ds(index * 128, 128), :] = part

def system_term(factor, cores):
    return pl.pallas_call(
        system_kernel,
        out_shape=jax.ShapeDtypeStruct((1280, 128), jnp.float32),
        in_specs=[pl.BlockSpec(memory_space=pltpu.VMEM)] * 2,
        out_specs=pl.BlockSpec(memory_space=pltpu.VMEM),
        scratch_shapes=[pltpu.VMEM((256, 256), jnp.float32)] * 5,
        compiler_params=pltpu.CompilerParams(vmem_limit_bytes=VM),
        cost_estimate=pl.CostEstimate(flops=6500000000, bytes_accessed=5000000, transcendentals=0),
    )(factor, cores)

def invert_block(m):
    rows = lax.broadcasted_iota(jnp.int32, (128, 128), 0)
    lanes = lax.broadcasted_iota(jnp.int32, (128, 128), 1)
    lane1 = lax.broadcasted_iota(jnp.int32, (1, 128), 1)
    for k in range(128):
        row = m[k:k + 1, :]
        col = m[:, k:k + 1]
        inv = 1.0 / m[k:k + 1, k:k + 1]
        scaled = jnp.where(lane1 == k, 1.0, row) * inv
        rest = jnp.where(lanes == k, 0.0, m)
        m = jnp.where(rows == k, scaled, rest - col * scaled)
    return m

def inverse_kernel(packed_ref, out_ref, blk_ref):
    index = 0
    for i in range(4):
        for j in range(i + 1):
            blk = packed_ref[pl.ds(index * 128, 128), :]
            if i == j:
                eye = lax.broadcasted_iota(jnp.int32, (128, 128), 0) == lax.broadcasted_iota(jnp.int32, (128, 128), 1)
                blk = blk + jnp.where(eye, 16.0, 0.0)
            out_ref[pl.ds(i * 128, 128), pl.ds(j * 128, 128)] = blk
            if i != j:
                out_ref[pl.ds(j * 128, 128), pl.ds(i * 128, 128)] = blk.T
            index += 1

    lane_block = lax.broadcasted_iota(jnp.int32, (512, 512), 1) // 128
    row_lane = lax.broadcasted_iota(jnp.int32, (128, 512), 1)
    sub_lane = lax.broadcasted_iota(jnp.int32, (128, 512), 0)

    def stage(p, carry):
        start = pl.multiple_of(p * 128, 128)
        col = out_ref[:, pl.ds(start, 128)]
        pivot = invert_block(out_ref[pl.ds(start, 128), pl.ds(start, 128)])
        row = out_ref[pl.ds(start, 128), :]
        eye = (row_lane - start == sub_lane).astype(jnp.float32)
        row = jnp.where(row_lane // 128 == p, eye, row)
        scaled = jnp.dot(pivot, row, precision=HI, preferred_element_type=jnp.float32)
        rest = jnp.where(lane_block == p, 0.0, out_ref[...])
        out_ref[...] = rest - jnp.dot(col, scaled, precision=HI, preferred_element_type=jnp.float32)
        out_ref[pl.ds(start, 128), :] = scaled
        return carry

    lax.fori_loop(0, 4, stage, 0)

def inverse(packed):
    return pl.pallas_call(
        inverse_kernel,
        out_shape=jax.ShapeDtypeStruct((512, 512), jnp.float32),
        in_specs=[pl.BlockSpec(memory_space=pltpu.VMEM)],
        out_specs=pl.BlockSpec(memory_space=pltpu.VMEM),
        scratch_shapes=[pltpu.VMEM((128, 128), jnp.float32)],
        compiler_params=pltpu.CompilerParams(vmem_limit_bytes=VM),
        cost_estimate=pl.CostEstimate(flops=3000000000, bytes_accessed=2000000, transcendentals=0),
    )(packed)

def align_kernel(rel_ref, block_ref, col_ref, flip_ref, values_ref, out_ref, place_ref, order_ref):
    def note(slot, carry):
        order_ref[col_ref[slot] // 2] = slot
        return carry

    lax.fori_loop(0, 64, note, 0)

    def move(index, carry):
        slot = jnp.where(index < 64, order_ref[jnp.minimum(index, 63)], index)
        flip = flip_ref[slot]
        place_ref[0, index] = col_ref[slot]
        place_ref[1, index] = flip * 8 + rel_ref[slot]
        place_ref[2, index] = block_ref[slot]
        tile = values_ref[slot]
        out_ref[index] = jnp.where(flip == 1, tile.T, tile)
        return carry

    lax.fori_loop(0, values_ref.shape[0], move, 0)


def align(tile_rel, tile_block, tile_col, tile_flip, values):
    slots = values.shape[0]
    scalar = pl.BlockSpec(memory_space=pltpu.SMEM)
    vector = pl.BlockSpec(memory_space=pltpu.VMEM)
    return pl.pallas_call(
        align_kernel,
        out_shape=(
            jax.ShapeDtypeStruct(values.shape, values.dtype),
            jax.ShapeDtypeStruct((3, slots), jnp.int32),
        ),
        in_specs=[scalar] * 4 + [vector],
        out_specs=(vector, scalar),
        scratch_shapes=[pltpu.SMEM((64,), jnp.int32)],
        compiler_params=pltpu.CompilerParams(vmem_limit_bytes=VM),
        cost_estimate=pl.CostEstimate(flops=100000000, bytes_accessed=4800000, transcendentals=0),
    )(tile_rel, tile_block, tile_col, tile_flip, values)


def rows_kernel(count_ref, place_ref, values_ref, panel_ref, core_ref, out_ref, sums_ref):
    chunk = pl.program_id(0)

    @pl.when(chunk == 0)
    def _():
        sums_ref[...] = jnp.zeros_like(sums_ref)

    def add(index, base):
        start = pl.multiple_of((place_ref[0, index] - base) * 128, 128)
        place = pl.multiple_of(place_ref[2, index] * 128, 128)
        term = jnp.dot(
            values_ref[index], panel_ref[pl.ds(start, 128), :], preferred_element_type=jnp.float32
        )
        where = (place_ref[1, index], pl.ds(place, 128), slice(None))
        sums_ref[where] = sums_ref[where] + term

    for owner in range(8):
        add(chunk * 8 + owner, chunk * 16)

    def extra(index, carry):
        @pl.when(place_ref[0, index] // 16 == chunk)
        def _():
            add(index, chunk * 16)

        return carry

    lax.fori_loop(64, count_ref[0], extra, 0)

    @pl.when(chunk == pl.num_programs(0) - 1)
    def _():
        out_ref[...] = jnp.zeros_like(out_ref)

        def relation(k, carry):
            core = core_ref[k]
            straight = sums_ref[k].astype(jnp.bfloat16)
            turned = sums_ref[k + 8].astype(jnp.bfloat16)
            out_ref[...] += dg(straight, core, 1, 1) + dg(turned, core, 1, 0)
            return carry

        lax.fori_loop(0, 8, relation, 0)


def partial_rows(count, place, values, panels, cores):
    slots = values.shape[0]
    return pl.pallas_call(
        rows_kernel,
        out_shape=jax.ShapeDtypeStruct((256, 512), jnp.float32),
        grid=(8,),
        in_specs=[
            pl.BlockSpec(memory_space=pltpu.SMEM),
            pl.BlockSpec(memory_space=pltpu.SMEM),
            pl.BlockSpec((slots, 128, 128), lambda i: (0, 0, 0)),
            pl.BlockSpec((2048, 512), lambda i: (i, 0)),
            pl.BlockSpec((8, 512, 512), lambda i: (0, 0, 0)),
        ],
        out_specs=pl.BlockSpec((256, 512), lambda i: (0, 0)),
        scratch_shapes=[pltpu.VMEM((16, 256, 512), jnp.float32)],
        compiler_params=pltpu.CompilerParams(vmem_limit_bytes=VM),
        cost_estimate=pl.CostEstimate(flops=5000000000, bytes_accessed=24000000, transcendentals=0),
    )(count, place, values, panels, cores)


def ent_shift(dx, dz, dc):
    pairs = []
    for x in range(4):
        for z in range(8):
            for c in range(2):
                there = (((x + dx) % 4) * 8 + (z + dz) % 8) * 2 + (c + dc) % 2
                pairs.append(((x * 8 + z) * 2 + c, there))
    return pairs


def ent_swap_z(bit):
    return [(e, e ^ (bit * 2)) for e in range(64)]


def rel_shift(d):
    return [(y, (y + d) % 4) for y in range(4)]


def scatter_sum(pieces, position, send):
    arrived = [send(lax.dynamic_index_in_dim(pieces, (position + d) % 4, 0, False), d) for d in (1, 2, 3)]
    own = lax.dynamic_index_in_dim(pieces, position, 0, False)
    return (own + arrived[1]) + (arrived[0] + arrived[2])


def gather(piece, position, send):
    parts = [piece] + [send(piece, d) for d in (1, 2, 3)]
    stack = jnp.stack(parts[:1] + parts[:0:-1] + parts[:1] + parts[:0:-1])
    return lax.dynamic_slice_in_dim(stack, (4 - position) % 4, 4, 0)


def sum_everywhere(packed):
    ent = lax.axis_index("ent")
    y = lax.axis_index("rel")
    x, core = ent // 16, ent % 2
    over_y = lambda v, d: lax.ppermute(v, "rel", rel_shift(d))
    over_x = lambda v, d: lax.ppermute(v, "ent", ent_shift(d, 0, 0))
    over_core = lambda v: lax.ppermute(v, "ent", ent_shift(0, 0, 1))
    halves = packed.reshape(2, 640, 128)
    part = lax.dynamic_index_in_dim(halves, core, 0, False) + over_core(
        lax.dynamic_index_in_dim(halves, 1 - core, 0, False)
    )
    part = scatter_sum(part.reshape(4, 160, 128), y, over_y)
    part = scatter_sum(part.reshape(4, 40, 128), x, over_x)
    for bit in (1, 2, 4):
        part = part + lax.ppermute(part, "ent", ent_swap_z(bit))
    part = gather(part, x, over_x).reshape(160, 128)
    part = gather(part, y, over_y).reshape(640, 128)
    other = over_core(part)
    first = jnp.where(core == 0, part, other)
    last = jnp.where(core == 0, other, part)
    return jnp.concatenate([first, last], axis=0)


def local(factor, core_tensors, tile_values, tile_rel, tile_block, tile_col, tile_flip, tile_count):
    panels = lax.all_gather(factor, "ent", tiled=True)
    system = sum_everywhere(system_term(factor, core_tensors))
    inverted = inverse(system)
    values, place = align(tile_rel[0], tile_block[0], tile_col[0], tile_flip[0], tile_values[0])
    rows = partial_rows(tile_count[0], place, values, panels, core_tensors)
    y = lax.axis_index("rel")
    over_y = lambda v, d: lax.ppermute(v, "rel", rel_shift(d))
    mine = scatter_sum(rows.reshape(4, 64, 512), y, over_y)
    updated = jnp.dot(mine, inverted, precision=HI)
    return gather(updated, y, over_y).reshape(256, 512)


def solution(mesh):
    in_specs = (
        P("ent", None),
        P("rel", None, None),
        P("rel", "ent", None, None),
        P("rel", "ent"),
        P("rel", "ent"),
        P("rel", "ent"),
        P("rel", "ent"),
        P("rel", "ent"),
    )
    out_specs = P("ent", None)
    return jax.shard_map(local, mesh=mesh, in_specs=in_specs, out_specs=out_specs, check_vma=False)
```

```python
import jax
import jax.numpy as jnp
from jax import lax
from jax.experimental import pallas as pl
from jax.experimental.pallas import tpu as pltpu
from jax.sharding import PartitionSpec as P

HIGHEST = lax.Precision.HIGHEST
MIB = 1024 * 1024
RIDGE = 16.0
IN_VMEM = pl.BlockSpec(memory_space=pltpu.VMEM)
IN_SMEM = pl.BlockSpec(memory_space=pltpu.SMEM)


def product(a, b, a_dim, b_dim):
    return lax.dot_general(a, b, (((a_dim,), (b_dim,)), ((), ())), preferred_element_type=jnp.float32)


def position():
    ent = lax.axis_index("ent")
    return ent // 16, lax.axis_index("rel"), ent % 2


def system_kernel(rows_ref, core_ref, out_ref, packed_ref, d0_ref, d1_ref, low_ref, c0_ref, c1_ref):
    rows = rows_ref[...]
    for ref in (d0_ref, d1_ref, low_ref, c0_ref, c1_ref):
        ref[...] = jnp.zeros_like(ref)

    def body(step, carry):
        core = core_ref[step]
        term = jnp.concatenate([product(rows, core, 1, 1), product(rows, core, 1, 0)], axis=0)
        high = term.astype(jnp.bfloat16)
        low = (term - high.astype(jnp.float32)).astype(jnp.bfloat16)
        h0, h1 = high[:, :256], high[:, 256:]
        l0, l1 = low[:, :256], low[:, 256:]
        h0t, h1t, l1t = h0.T, h1.T, l1.T
        d0_ref[...] += product(h0t, h0, 1, 0)
        d1_ref[...] += product(h1t, h1, 1, 0)
        c0_ref[...] += product(h0t, l0, 1, 0)
        c1_ref[...] += product(h1t, l1, 1, 0)
        low_ref[...] += product(h1t, h0, 1, 0) + product(h1t, l0, 1, 0) + product(l1t, h0, 1, 0)
        return carry

    lax.fori_loop(0, core_ref.shape[0], body, 0)
    first = d0_ref[...] + (c0_ref[...] + c0_ref[...].T)
    last = d1_ref[...] + (c1_ref[...] + c1_ref[...].T)
    mixed = low_ref[...]
    blocks = (
        first[:128, :128], first[128:, :128], first[128:, 128:],
        mixed[:128, :128], mixed[:128, 128:], last[:128, :128],
        mixed[128:, :128], mixed[128:, 128:], last[128:, :128], last[128:, 128:],
    )
    for index, block in enumerate(blocks):
        packed_ref[pl.ds(index * 128, 128), :] = block
    x, y, core = position()
    for c in range(2):
        for j in range(4):
            for k in range(4):
                start = ((c + core) % 2) * 640 + ((j - y + 4) % 4) * 160 + ((k - x + 4) % 4) * 40
                out_ref[pl.ds(pl.multiple_of(start, 8), 40), :] = packed_ref[pl.ds(c * 640 + j * 160 + k * 40, 40), :]


def system_term(factor, cores):
    return pl.pallas_call(
        system_kernel,
        out_shape=jax.ShapeDtypeStruct((1280, 128), jnp.float32),
        in_specs=[IN_VMEM] * 2,
        out_specs=IN_VMEM,
        scratch_shapes=[pltpu.VMEM((1280, 128), jnp.float32)] + [pltpu.VMEM((256, 256), jnp.float32)] * 5,
        compiler_params=pltpu.CompilerParams(vmem_limit_bytes=32 * MIB),
        cost_estimate=pl.CostEstimate(flops=12000000000, bytes_accessed=5000000, transcendentals=0),
    )(factor, cores)


def invert_block(m):
    full = (8, 128)
    blocks = [m[8 * r:8 * r + 8, :] for r in range(16)]
    lanes = lax.broadcasted_iota(jnp.int32, full, 1)
    subs = lax.broadcasted_iota(jnp.int32, full, 0)
    for q in range(16):
        panel = blocks[q]
        d = {
            (i, j): jnp.broadcast_to(panel[i:i + 1, 8 * q + j:8 * q + j + 1], full)
            for i in range(8)
            for j in range(i + 1)
        }
        entry = lambda i, j: d[max(i, j), min(i, j)]
        for k in range(8):
            inverse = 1.0 / d[k, k]
            ratio = {i: entry(i, k) * inverse for i in range(8) if i != k}
            for i in range(8):
                for j in range(i + 1):
                    if i != k and j != k:
                        d[i, j] = d[i, j] - ratio[i] * entry(j, k)
            for i in ratio:
                d[max(i, k), min(i, k)] = ratio[i]
            d[k, k] = -inverse
        inside = lanes // 8 == q
        unit = [
            jnp.broadcast_to(
                jnp.where(inside, (lanes == 8 * q + j).astype(jnp.float32), panel)[j:j + 1, :], full
            )
            for j in range(8)
        ]
        scaled = []
        for i in range(8):
            row = entry(i, 0) * unit[0]
            for j in range(1, 8):
                row = row + entry(i, j) * unit[j]
            scaled.append(row)
        for r in range(16):
            if r != q:
                old = blocks[r]
                new = jnp.where(inside, 0.0, old)
                for i in range(8):
                    new = new + jnp.broadcast_to(old[:, 8 * q + i:8 * q + i + 1], full) * scaled[i]
                blocks[r] = new
        row = scaled[0]
        for i in range(1, 8):
            row = jnp.where(subs == i, scaled[i], row)
        blocks[q] = -row
    return jnp.concatenate(blocks, axis=0)


def inverse_kernel(own_ref, other_ref, out_ref, packed_ref):
    x, y, core = position()
    for i, part_ref in enumerate((own_ref, other_ref)):
        for j in range(4):
            for k in range(4):
                start = ((core + i) % 2) * 640 + ((y - j + 4) % 4) * 160 + ((x - k + 4) % 4) * 40
                packed_ref[pl.ds(pl.multiple_of(start, 8), 40), :] = part_ref[pl.ds(j * 160 + k * 40, 40), :]
    eye = lax.broadcasted_iota(jnp.int32, (128, 128), 0) == lax.broadcasted_iota(jnp.int32, (128, 128), 1)
    index = 0
    for i in range(4):
        for j in range(i + 1):
            block = packed_ref[pl.ds(index * 128, 128), :]
            if i == j:
                block = block + jnp.where(eye, RIDGE, 0.0)
            else:
                out_ref[pl.ds(j * 128, 128), pl.ds(i * 128, 128)] = block.T
            out_ref[pl.ds(i * 128, 128), pl.ds(j * 128, 128)] = block
            index += 1
    lane_block = lax.broadcasted_iota(jnp.int32, (512, 512), 1) // 128
    row_lane = lax.broadcasted_iota(jnp.int32, (128, 512), 1)
    row_sub = lax.broadcasted_iota(jnp.int32, (128, 512), 0)

    def stage(p, carry):
        start = pl.multiple_of(p * 128, 128)
        part = pl.ds(start, 128)
        column = out_ref[:, part]
        pivot = invert_block(out_ref[part, part])
        row = jnp.where(row_lane // 128 == p, (row_lane - start == row_sub).astype(jnp.float32), out_ref[part, :])
        scaled = jnp.dot(pivot, row, precision=HIGHEST, preferred_element_type=jnp.float32)
        rest = jnp.where(lane_block == p, 0.0, out_ref[...])
        out_ref[...] = rest - jnp.dot(column, scaled, precision=HIGHEST, preferred_element_type=jnp.float32)
        out_ref[part, :] = scaled
        return carry

    lax.fori_loop(0, 4, stage, 0)


def inverse(own, other):
    return pl.pallas_call(
        inverse_kernel,
        out_shape=jax.ShapeDtypeStruct((512, 512), jnp.float32),
        in_specs=[IN_VMEM] * 2,
        out_specs=IN_VMEM,
        scratch_shapes=[pltpu.VMEM((1280, 128), jnp.float32)],
        compiler_params=pltpu.CompilerParams(vmem_limit_bytes=32 * MIB),
        cost_estimate=pl.CostEstimate(flops=30000000000, bytes_accessed=2000000, transcendentals=0),
    )(own, other)


def align_kernel(rel_ref, block_ref, col_ref, flip_ref, values_ref, out_ref, place_ref, order_ref):
    def note(slot, carry):
        order_ref[col_ref[slot] // 2] = slot
        return carry

    lax.fori_loop(0, 64, note, 0)

    def move(step, carry):
        for i in range(8):
            index = step * 8 + i
            slot = jnp.where(index < 64, order_ref[jnp.minimum(index, 63)], index)
            flip = flip_ref[slot]
            place_ref[0, index] = col_ref[slot]
            place_ref[1, index] = flip * 8 + rel_ref[slot]
            place_ref[2, index] = block_ref[slot]
            tile = values_ref[slot]
            out_ref[index] = jnp.where(flip == 1, tile.T, tile)
        return carry

    lax.fori_loop(0, values_ref.shape[0] // 8, move, 0)


def align(tile_rel, tile_block, tile_col, tile_flip, values):
    slots = values.shape[0]
    return pl.pallas_call(
        align_kernel,
        out_shape=(
            jax.ShapeDtypeStruct(values.shape, values.dtype),
            jax.ShapeDtypeStruct((3, slots), jnp.int32),
        ),
        in_specs=[IN_SMEM] * 4 + [IN_VMEM],
        out_specs=(IN_VMEM, IN_SMEM),
        scratch_shapes=[pltpu.SMEM((64,), jnp.int32)],
        compiler_params=pltpu.CompilerParams(vmem_limit_bytes=16 * MIB),
        cost_estimate=pl.CostEstimate(flops=3000000000, bytes_accessed=4800000, transcendentals=0),
    )(tile_rel, tile_block, tile_col, tile_flip, values)


def rows_kernel(count_ref, place_ref, values_ref, cores_ref, panels_ref, out_ref, sums_ref, panel_ref, core_ref, sem, core_sem):
    def fetch(owner):
        start = pl.multiple_of(place_ref[0, owner] * 128, 128)
        return pltpu.make_async_copy(panels_ref.at[pl.ds(start, 128), :], panel_ref.at[owner], sem.at[owner])

    def begin(step, carry):
        for i in range(8):
            fetch(step * 8 + i).start()
        return carry

    lax.fori_loop(0, 8, begin, 0)
    core_copy = pltpu.make_async_copy(cores_ref, core_ref, core_sem)
    core_copy.start()
    sums_ref[...] = jnp.zeros_like(sums_ref)

    def add(index, owner):
        place = pl.multiple_of(place_ref[2, index] * 128, 128)
        term = product(values_ref[index], panel_ref[owner], 1, 0)
        where = (place_ref[1, index], pl.ds(place, 128), slice(None))
        sums_ref[where] = sums_ref[where] + term

    def main(step, carry):
        for i in range(8):
            fetch(step * 8 + i).wait()
        for i in range(8):
            add(step * 8 + i, step * 8 + i)
        return carry

    lax.fori_loop(0, 8, main, 0)

    def extra(index, carry):
        add(index, place_ref[0, index] // 2)
        return carry

    lax.fori_loop(64, count_ref[0], extra, 0)
    core_copy.wait()
    total = jnp.zeros(out_ref.shape, jnp.float32)
    for k in range(8):
        core = core_ref[k]
        total += product(sums_ref[k].astype(jnp.bfloat16), core, 1, 1)
        total += product(sums_ref[k + 8].astype(jnp.bfloat16), core, 1, 0)
    out_ref[...] = total.astype(out_ref.dtype)


def partial_rows(count, place, values, cores, panels):
    return pl.pallas_call(
        rows_kernel,
        out_shape=jax.ShapeDtypeStruct((256, 512), jnp.bfloat16),
        in_specs=[IN_SMEM, IN_SMEM, IN_VMEM] + [pl.BlockSpec(memory_space=pl.ANY)] * 2,
        out_specs=IN_VMEM,
        scratch_shapes=[
            pltpu.VMEM((16, 256, 512), jnp.float32),
            pltpu.VMEM((64, 128, 512), jnp.bfloat16),
            pltpu.VMEM(cores.shape, cores.dtype),
            pltpu.SemaphoreType.DMA((64,)),
            pltpu.SemaphoreType.DMA,
        ],
        compiler_params=pltpu.CompilerParams(vmem_limit_bytes=40 * MIB),
        cost_estimate=pl.CostEstimate(flops=10000000000, bytes_accessed=16000000, transcendentals=0),
    )(count, place, values, cores, panels)


def finish_kernel(own_ref, first_ref, second_ref, third_ref, inverse_ref, out_ref):
    wide = lambda ref: ref[...].astype(jnp.float32)
    rows = (wide(own_ref) + wide(second_ref)) + (wide(first_ref) + wide(third_ref))
    out_ref[...] = jnp.dot(rows, inverse_ref[...], precision=HIGHEST, preferred_element_type=jnp.float32)


def finish(own, arrived, inverted):
    return pl.pallas_call(
        finish_kernel,
        out_shape=jax.ShapeDtypeStruct(own.shape, jnp.float32),
        in_specs=[IN_VMEM] * 5,
        out_specs=IN_VMEM,
        compiler_params=pltpu.CompilerParams(vmem_limit_bytes=16 * MIB),
        cost_estimate=pl.CostEstimate(flops=1000000000, bytes_accessed=2500000, transcendentals=0),
    )(own, *arrived, inverted)


def over_y(v, d):
    return lax.ppermute(v, "rel", [(y, (y + d) % 4) for y in range(4)])


def over_x(v, d):
    return lax.ppermute(v, "ent", [(e, (e + 16 * d) % 64) for e in range(64)])


def swap_z(v, bits):
    return lax.ppermute(v, "ent", [(e, e ^ (2 * bits)) for e in range(64)])


def swap_core(v):
    return lax.ppermute(v, "ent", [(e, e ^ 1) for e in range(64)])


def scatter_sum(part, send):
    quarter = part.shape[0] // 4
    arrived = [send(part[d * quarter:(d + 1) * quarter], d) for d in (1, 2, 3)]
    return (part[:quarter] + arrived[1]) + (arrived[0] + arrived[2])


def gather(part, send):
    return jnp.concatenate([part] + [send(part, d) for d in (1, 2, 3)], axis=0)


def sum_everywhere(placed):
    part = placed[:640] + swap_core(placed[640:])
    part = scatter_sum(part, over_y)
    part = scatter_sum(part, over_x)
    part = part + swap_z(part, 1)
    arrived = [swap_z(part, bits) for bits in (2, 4, 6)]
    part = (part + arrived[1]) + (arrived[0] + arrived[2])
    part = gather(gather(part, over_x), over_y)
    return part, swap_core(part)


def local(factor, core_tensors, tile_values, tile_rel, tile_block, tile_col, tile_flip, tile_count):
    panels = lax.all_gather(factor, "ent", tiled=True)
    inverted = inverse(*sum_everywhere(system_term(factor, core_tensors)))
    values, place = align(tile_rel[0], tile_block[0], tile_col[0], tile_flip[0], tile_values[0])
    panels, inverted, values, place = lax.optimization_barrier((panels, inverted, values, place))
    rows = partial_rows(tile_count[0], place, values, core_tensors, panels)
    return finish(rows, [over_y(rows, d) for d in (1, 2, 3)], inverted)


def solution(mesh):
    in_specs = (
        P("ent", None),
        P("rel", None, None),
        P("rel", "ent", None, None),
        P("rel", "ent"),
        P("rel", "ent"),
        P("rel", "ent"),
        P("rel", "ent"),
        P("rel", "ent"),
    )
    out_specs = P("ent", None)
    return jax.shard_map(local, mesh=mesh, in_specs=in_specs, out_specs=out_specs, check_vma=False)
```

```python
import jax
import jax.numpy as jnp
from jax import lax
from jax.experimental import pallas as pl
from jax.experimental.pallas import tpu as pltpu
from jax.sharding import PartitionSpec as P

HIGHEST = lax.Precision.HIGHEST
MIB = 1024 * 1024
RIDGE = 16.0
IN_VMEM = pl.BlockSpec(memory_space=pltpu.VMEM)
IN_SMEM = pl.BlockSpec(memory_space=pltpu.SMEM)


def product(a, b, a_dim, b_dim):
    return lax.dot_general(a, b, (((a_dim,), (b_dim,)), ((), ())), preferred_element_type=jnp.float32)


def position():
    ent = lax.axis_index("ent")
    return ent // 16, lax.axis_index("rel"), ent % 2


def system_kernel(rows_ref, core_ref, out_ref, packed_ref, d0_ref, d1_ref, low_ref, c0_ref, c1_ref):
    rows = rows_ref[...]
    for ref in (d0_ref, d1_ref, low_ref, c0_ref, c1_ref):
        ref[...] = jnp.zeros_like(ref)

    def body(step, carry):
        core = core_ref[step]
        term = jnp.concatenate([product(rows, core, 1, 1), product(rows, core, 1, 0)], axis=0)
        high = term.astype(jnp.bfloat16)
        low = (term - high.astype(jnp.float32)).astype(jnp.bfloat16)
        h0, h1 = high[:, :256], high[:, 256:]
        l0, l1 = low[:, :256], low[:, 256:]
        h0t, h1t, l1t = h0.T, h1.T, l1.T
        d0_ref[...] += product(h0t, h0, 1, 0)
        d1_ref[...] += product(h1t, h1, 1, 0)
        c0_ref[...] += product(h0t, l0, 1, 0)
        c1_ref[...] += product(h1t, l1, 1, 0)
        low_ref[...] += product(h1t, h0, 1, 0) + product(h1t, l0, 1, 0) + product(l1t, h0, 1, 0)
        return carry

    lax.fori_loop(0, core_ref.shape[0], body, 0)
    first = d0_ref[...] + (c0_ref[...] + c0_ref[...].T)
    last = d1_ref[...] + (c1_ref[...] + c1_ref[...].T)
    mixed = low_ref[...]
    blocks = (
        first[:128, :128], first[128:, :128], first[128:, 128:],
        mixed[:128, :128], mixed[:128, 128:], last[:128, :128],
        mixed[128:, :128], mixed[128:, 128:], last[128:, :128], last[128:, 128:],
    )
    for index, block in enumerate(blocks):
        packed_ref[pl.ds(index * 128, 128), :] = block
    x, y, core = position()
    for c in range(2):
        for j in range(4):
            for k in range(4):
                start = ((c + core) % 2) * 640 + ((j - y + 4) % 4) * 160 + ((k - x + 4) % 4) * 40
                out_ref[pl.ds(pl.multiple_of(start, 8), 40), :] = packed_ref[pl.ds(c * 640 + j * 160 + k * 40, 40), :]


def system_term(factor, cores):
    return pl.pallas_call(
        system_kernel,
        out_shape=jax.ShapeDtypeStruct((1280, 128), jnp.float32),
        in_specs=[IN_VMEM] * 2,
        out_specs=IN_VMEM,
        scratch_shapes=[pltpu.VMEM((1280, 128), jnp.float32)] + [pltpu.VMEM((256, 256), jnp.float32)] * 5,
        compiler_params=pltpu.CompilerParams(vmem_limit_bytes=32 * MIB),
        cost_estimate=pl.CostEstimate(flops=12000000000, bytes_accessed=5000000, transcendentals=0),
    )(factor, cores)


def invert_block(m):
    full = (8, 128)
    blocks = [m[8 * r:8 * r + 8, :] for r in range(16)]
    lanes = lax.broadcasted_iota(jnp.int32, full, 1)
    subs = lax.broadcasted_iota(jnp.int32, full, 0)
    for q in range(16):
        panel = blocks[q]
        d = {
            (i, j): jnp.broadcast_to(panel[i:i + 1, 8 * q + j:8 * q + j + 1], full)
            for i in range(8)
            for j in range(i + 1)
        }
        entry = lambda i, j: d[max(i, j), min(i, j)]
        for k in range(8):
            inverse = 1.0 / d[k, k]
            ratio = {i: entry(i, k) * inverse for i in range(8) if i != k}
            for i in range(8):
                for j in range(i + 1):
                    if i != k and j != k:
                        d[i, j] = d[i, j] - ratio[i] * entry(j, k)
            for i in ratio:
                d[max(i, k), min(i, k)] = ratio[i]
            d[k, k] = -inverse
        inside = lanes // 8 == q
        unit = [
            jnp.broadcast_to(
                jnp.where(inside, (lanes == 8 * q + j).astype(jnp.float32), panel)[j:j + 1, :], full
            )
            for j in range(8)
        ]
        scaled = []
        for i in range(8):
            row = entry(i, 0) * unit[0]
            for j in range(1, 8):
                row = row + entry(i, j) * unit[j]
            scaled.append(row)
        for r in range(16):
            if r != q:
                old = blocks[r]
                new = jnp.where(inside, 0.0, old)
                for i in range(8):
                    new = new + jnp.broadcast_to(old[:, 8 * q + i:8 * q + i + 1], full) * scaled[i]
                blocks[r] = new
        row = scaled[0]
        for i in range(1, 8):
            row = jnp.where(subs == i, scaled[i], row)
        blocks[q] = -row
    return jnp.concatenate(blocks, axis=0)


def inverse_kernel(own_ref, other_ref, out_ref, packed_ref):
    x, y, core = position()
    for i, part_ref in enumerate((own_ref, other_ref)):
        for j in range(4):
            for k in range(4):
                start = ((core + i) % 2) * 640 + ((y - j + 4) % 4) * 160 + ((x - k + 4) % 4) * 40
                packed_ref[pl.ds(pl.multiple_of(start, 8), 40), :] = part_ref[pl.ds(j * 160 + k * 40, 40), :]
    eye = lax.broadcasted_iota(jnp.int32, (128, 128), 0) == lax.broadcasted_iota(jnp.int32, (128, 128), 1)
    index = 0
    for i in range(4):
        for j in range(i + 1):
            block = packed_ref[pl.ds(index * 128, 128), :]
            if i == j:
                block = block + jnp.where(eye, RIDGE, 0.0)
            else:
                out_ref[pl.ds(j * 128, 128), pl.ds(i * 128, 128)] = block.T
            out_ref[pl.ds(i * 128, 128), pl.ds(j * 128, 128)] = block
            index += 1
    lane_block = lax.broadcasted_iota(jnp.int32, (512, 512), 1) // 128
    row_lane = lax.broadcasted_iota(jnp.int32, (128, 512), 1)
    row_sub = lax.broadcasted_iota(jnp.int32, (128, 512), 0)

    def stage(p, carry):
        start = pl.multiple_of(p * 128, 128)
        part = pl.ds(start, 128)
        column = out_ref[:, part]
        pivot = invert_block(out_ref[part, part])
        row = jnp.where(row_lane // 128 == p, (row_lane - start == row_sub).astype(jnp.float32), out_ref[part, :])
        scaled = jnp.dot(pivot, row, precision=HIGHEST, preferred_element_type=jnp.float32)
        rest = jnp.where(lane_block == p, 0.0, out_ref[...])
        out_ref[...] = rest - jnp.dot(column, scaled, precision=HIGHEST, preferred_element_type=jnp.float32)
        out_ref[part, :] = scaled
        return carry

    lax.fori_loop(0, 4, stage, 0)


def inverse(own, other):
    return pl.pallas_call(
        inverse_kernel,
        out_shape=jax.ShapeDtypeStruct((512, 512), jnp.float32),
        in_specs=[IN_VMEM] * 2,
        out_specs=IN_VMEM,
        scratch_shapes=[pltpu.VMEM((1280, 128), jnp.float32)],
        compiler_params=pltpu.CompilerParams(vmem_limit_bytes=32 * MIB),
        cost_estimate=pl.CostEstimate(flops=30000000000, bytes_accessed=2000000, transcendentals=0),
    )(own, other)


def align_kernel(rel_ref, block_ref, col_ref, flip_ref, values_ref, out_ref, place_ref, order_ref):
    def note(slot, carry):
        order_ref[col_ref[slot] // 2] = slot
        return carry

    lax.fori_loop(0, 64, note, 0)

    def move(step, carry):
        for i in range(8):
            index = step * 8 + i
            slot = jnp.where(index < 64, order_ref[jnp.minimum(index, 63)], index)
            flip = flip_ref[slot]
            place_ref[0, index] = col_ref[slot]
            place_ref[1, index] = flip * 8 + rel_ref[slot]
            place_ref[2, index] = block_ref[slot]
            tile = values_ref[slot]
            out_ref[index] = jnp.where(flip == 1, tile.T, tile)
        return carry

    lax.fori_loop(0, values_ref.shape[0] // 8, move, 0)


def align(tile_rel, tile_block, tile_col, tile_flip, values):
    slots = values.shape[0]
    return pl.pallas_call(
        align_kernel,
        out_shape=(
            jax.ShapeDtypeStruct(values.shape, values.dtype),
            jax.ShapeDtypeStruct((3, slots), jnp.int32),
        ),
        in_specs=[IN_SMEM] * 4 + [IN_VMEM],
        out_specs=(pl.BlockSpec(memory_space=pltpu.VMEM), IN_SMEM),
        scratch_shapes=[pltpu.SMEM((64,), jnp.int32)],
        compiler_params=pltpu.CompilerParams(vmem_limit_bytes=16 * MIB),
        cost_estimate=pl.CostEstimate(flops=3000000000, bytes_accessed=4800000, transcendentals=0),
    )(tile_rel, tile_block, tile_col, tile_flip, values)


def rows_kernel(
    count_ref, place_ref, tiles_ref, cores_ref, panels_ref, upper_ref, lower_ref, sums_ref, panel_ref, core_ref, values_ref,
    sem, core_sem, values_sem
):
    def fetch(owner):
        start = pl.multiple_of(place_ref[0, owner] * 128, 128)
        return pltpu.make_async_copy(panels_ref.at[pl.ds(start, 128), :], panel_ref.at[owner], sem.at[owner])

    values_copy = pltpu.make_async_copy(tiles_ref, values_ref, values_sem)
    values_copy.start()

    def begin(step, carry):
        for i in range(8):
            fetch(step * 8 + i).start()
        return carry

    lax.fori_loop(0, 8, begin, 0)
    core_copy = pltpu.make_async_copy(cores_ref, core_ref, core_sem)
    core_copy.start()
    sums_ref[...] = jnp.zeros_like(sums_ref)

    def add(index, owner):
        place = pl.multiple_of(place_ref[2, index] * 128, 128)
        term = product(values_ref[index], panel_ref[owner], 1, 0)
        where = (place_ref[1, index], pl.ds(place, 128), slice(None))
        sums_ref[where] = sums_ref[where] + term

    values_copy.wait()

    def main(step, carry):
        for i in range(8):
            fetch(step * 8 + i).wait()
        for i in range(8):
            add(step * 8 + i, step * 8 + i)
        return carry

    lax.fori_loop(0, 8, main, 0)

    def extra(index, carry):
        add(index, place_ref[0, index] // 2)
        return carry

    lax.fori_loop(64, count_ref[0], extra, 0)
    core_copy.wait()
    total = jnp.zeros((256, 512), jnp.float32)
    for k in range(8):
        core = core_ref[k]
        total += product(sums_ref[k].astype(jnp.bfloat16), core, 1, 1)
        total += product(sums_ref[k + 8].astype(jnp.bfloat16), core, 1, 0)
    rounded = total.astype(jnp.bfloat16)
    upper_ref[...] = rounded[:128]
    lower_ref[...] = rounded[128:]


def partial_rows(count, place, values, cores, panels):
    return pl.pallas_call(
        rows_kernel,
        out_shape=(jax.ShapeDtypeStruct((128, 512), jnp.bfloat16),) * 2,
        in_specs=[IN_SMEM, IN_SMEM] + [pl.BlockSpec(memory_space=pltpu.HBM)] * 3,
        out_specs=(IN_VMEM,) * 2,
        scratch_shapes=[
            pltpu.VMEM((16, 256, 512), jnp.float32),
            pltpu.VMEM((64, 128, 512), jnp.bfloat16),
            pltpu.VMEM(cores.shape, cores.dtype),
            pltpu.VMEM(values.shape, values.dtype),
            pltpu.SemaphoreType.DMA((64,)),
            pltpu.SemaphoreType.DMA,
            pltpu.SemaphoreType.DMA,
        ],
        compiler_params=pltpu.CompilerParams(vmem_limit_bytes=60 * MIB),
        cost_estimate=pl.CostEstimate(flops=10000000000, bytes_accessed=16000000, transcendentals=0),
    )(count, place, values, cores, panels)


def finish_kernel(upper_ref, upper_other_ref, lower_ref, lower_other_ref, inverse_ref, out_ref):
    wide = lambda ref: ref[...].astype(jnp.float32)
    upper = wide(upper_ref) + wide(upper_other_ref)
    lower = wide(lower_ref) + wide(lower_other_ref)
    rows = jnp.concatenate([upper, lower], axis=0)
    out_ref[...] = jnp.dot(rows, inverse_ref[...], precision=HIGHEST, preferred_element_type=jnp.float32)


def finish(upper, upper_other, lower, lower_other, inverted):
    return pl.pallas_call(
        finish_kernel,
        out_shape=jax.ShapeDtypeStruct((256, 512), jnp.float32),
        in_specs=[IN_VMEM] * 5,
        out_specs=IN_VMEM,
        compiler_params=pltpu.CompilerParams(vmem_limit_bytes=16 * MIB),
        cost_estimate=pl.CostEstimate(flops=1000000000, bytes_accessed=2500000, transcendentals=0),
    )(upper, upper_other, lower, lower_other, inverted)


def over_y(v, d):
    return lax.ppermute(v, "rel", [(y, (y + d) % 4) for y in range(4)])


def swap_y(v, bits):
    return lax.ppermute(v, "rel", [(y, y ^ bits) for y in range(4)])


def over_x(v, d):
    return lax.ppermute(v, "ent", [(e, (e + 16 * d) % 64) for e in range(64)])


def swap_z(v, bits):
    return lax.ppermute(v, "ent", [(e, e ^ (2 * bits)) for e in range(64)])


def swap_core(v):
    return lax.ppermute(v, "ent", [(e, e ^ 1) for e in range(64)])


def scatter_sum(part, send):
    quarter = part.shape[0] // 4
    arrived = [send(part[d * quarter:(d + 1) * quarter], d) for d in (1, 2, 3)]
    return (part[:quarter] + arrived[1]) + (arrived[0] + arrived[2])


def gather(part, send):
    return jnp.concatenate([part] + [send(part, d) for d in (1, 2, 3)], axis=0)


def sum_everywhere(placed):
    part = placed[:640] + swap_core(placed[640:])
    part = scatter_sum(part, over_y)
    part = scatter_sum(part, over_x)
    part = part + swap_z(part, 1)
    arrived = [swap_z(part, bits) for bits in (2, 4, 6)]
    part = (part + arrived[1]) + (arrived[0] + arrived[2])
    part = gather(gather(part, over_x), over_y)
    return part, swap_core(part)


def local(factor, core_tensors, tile_values, tile_rel, tile_block, tile_col, tile_flip, tile_count):
    panels = lax.all_gather(factor, "ent", tiled=True)
    inverted = inverse(*sum_everywhere(system_term(factor, core_tensors)))
    values, place = align(tile_rel[0], tile_block[0], tile_col[0], tile_flip[0], tile_values[0])
    panels, inverted, values, place = lax.optimization_barrier((panels, inverted, values, place))
    upper, lower = partial_rows(tile_count[0], place, values, core_tensors, panels)
    add = lambda a, b: (a.astype(jnp.float32) + b.astype(jnp.float32)).astype(jnp.bfloat16)
    upper, lower = add(upper, swap_y(upper, 1)), add(lower, swap_y(lower, 3))
    return finish(upper, swap_y(upper, 3), lower, swap_y(lower, 1), inverted)


def solution(mesh):
    in_specs = (
        P("ent", None),
        P("rel", None, None),
        P("rel", "ent", None, None),
        P("rel", "ent"),
        P("rel", "ent"),
        P("rel", "ent"),
        P("rel", "ent"),
        P("rel", "ent"),
    )
    out_specs = P("ent", None)
    return jax.shard_map(local, mesh=mesh, in_specs=in_specs, out_specs=out_specs, check_vma=False)
```

```python
import jax
import jax.numpy as jnp
from jax import lax
from jax.experimental import pallas as pl
from jax.experimental.pallas import tpu as pltpu
from jax.sharding import PartitionSpec as P

HIGHEST = lax.Precision.HIGHEST
MIB = 1024 * 1024
RIDGE = 16.0
IN_VMEM = pl.BlockSpec(memory_space=pltpu.VMEM)
IN_SMEM = pl.BlockSpec(memory_space=pltpu.SMEM)


def product(a, b, a_dim, b_dim):
    return lax.dot_general(a, b, (((a_dim,), (b_dim,)), ((), ())), preferred_element_type=jnp.float32)


def position():
    ent = lax.axis_index("ent")
    return ent // 16, lax.axis_index("rel"), ent % 2


def system_kernel(rows_ref, cores_ref, out_ref, core_ref, packed_ref, d0_ref, d1_ref, low_ref, c0_ref, c1_ref, sem):
    fetch = lambda step: pltpu.make_async_copy(cores_ref.at[step], core_ref.at[step], sem.at[step])
    for step in range(8):
        fetch(step).start()
    rows = rows_ref[...]
    for ref in (d0_ref, d1_ref, low_ref, c0_ref, c1_ref):
        ref[...] = jnp.zeros_like(ref)

    def body(step, carry):
        fetch(step).wait()
        core = core_ref[step]
        term = jnp.concatenate([product(rows, core, 1, 1), product(rows, core, 1, 0)], axis=0)
        high = term.astype(jnp.bfloat16)
        low = (term - high.astype(jnp.float32)).astype(jnp.bfloat16)
        h0, h1 = high[:, :256], high[:, 256:]
        l0, l1 = low[:, :256], low[:, 256:]
        h0t, h1t, l1t = h0.T, h1.T, l1.T
        d0_ref[...] += product(h0t, h0, 1, 0)
        d1_ref[...] += product(h1t, h1, 1, 0)
        c0_ref[...] += product(h0t, l0, 1, 0)
        c1_ref[...] += product(h1t, l1, 1, 0)
        low_ref[...] += product(h1t, h0, 1, 0) + product(h1t, l0, 1, 0) + product(l1t, h0, 1, 0)
        return carry

    lax.fori_loop(0, core_ref.shape[0], body, 0)
    first = d0_ref[...] + (c0_ref[...] + c0_ref[...].T)
    last = d1_ref[...] + (c1_ref[...] + c1_ref[...].T)
    mixed = low_ref[...]
    blocks = (
        first[:128, :128], first[128:, :128], first[128:, 128:],
        mixed[:128, :128], mixed[:128, 128:], last[:128, :128],
        mixed[128:, :128], mixed[128:, 128:], last[128:, :128], last[128:, 128:],
    )
    for index, block in enumerate(blocks):
        packed_ref[pl.ds(index * 128, 128), :] = block
    x, y, core = position()
    for c in range(2):
        for j in range(4):
            for k in range(4):
                start = ((c + core) % 2) * 640 + ((j - y + 4) % 4) * 160 + ((k - x + 4) % 4) * 40
                out_ref[pl.ds(pl.multiple_of(start, 8), 40), :] = packed_ref[pl.ds(c * 640 + j * 160 + k * 40, 40), :]


def system_term(factor, cores):
    return pl.pallas_call(
        system_kernel,
        out_shape=jax.ShapeDtypeStruct((1280, 128), jnp.float32),
        in_specs=[IN_VMEM, pl.BlockSpec(memory_space=pltpu.HBM)],
        out_specs=IN_VMEM,
        scratch_shapes=[pltpu.VMEM(cores.shape, cores.dtype), pltpu.VMEM((1280, 128), jnp.float32)]
        + [pltpu.VMEM((256, 256), jnp.float32)] * 5
        + [pltpu.SemaphoreType.DMA((8,))],
        compiler_params=pltpu.CompilerParams(vmem_limit_bytes=52 * MIB),
        cost_estimate=pl.CostEstimate(flops=12000000000, bytes_accessed=5000000, transcendentals=0),
    )(factor, cores)


def invert_block(m):
    full = (8, 128)
    blocks = [m[8 * r:8 * r + 8, :] for r in range(16)]
    lanes = lax.broadcasted_iota(jnp.int32, full, 1)
    subs = lax.broadcasted_iota(jnp.int32, full, 0)
    for q in range(16):
        panel = blocks[q]
        d = {
            (i, j): jnp.broadcast_to(panel[i:i + 1, 8 * q + j:8 * q + j + 1], full)
            for i in range(8)
            for j in range(i + 1)
        }
        entry = lambda i, j: d[max(i, j), min(i, j)]
        for k in range(8):
            inverse = 1.0 / d[k, k]
            ratio = {i: entry(i, k) * inverse for i in range(8) if i != k}
            for i in range(8):
                for j in range(i + 1):
                    if i != k and j != k:
                        d[i, j] = d[i, j] - ratio[i] * entry(j, k)
            for i in ratio:
                d[max(i, k), min(i, k)] = ratio[i]
            d[k, k] = -inverse
        inside = lanes // 8 == q
        unit = [
            jnp.broadcast_to(
                jnp.where(inside, (lanes == 8 * q + j).astype(jnp.float32), panel)[j:j + 1, :], full
            )
            for j in range(8)
        ]
        scaled = []
        for i in range(8):
            row = entry(i, 0) * unit[0]
            for j in range(1, 8):
                row = row + entry(i, j) * unit[j]
            scaled.append(row)
        for r in range(16):
            if r != q:
                old = blocks[r]
                new = jnp.where(inside, 0.0, old)
                for i in range(8):
                    new = new + jnp.broadcast_to(old[:, 8 * q + i:8 * q + i + 1], full) * scaled[i]
                blocks[r] = new
        row = scaled[0]
        for i in range(1, 8):
            row = jnp.where(subs == i, scaled[i], row)
        blocks[q] = -row
    return jnp.concatenate(blocks, axis=0)


def inverse_kernel(own_ref, other_ref, out_ref, packed_ref):
    x, y, core = position()
    for i, part_ref in enumerate((own_ref, other_ref)):
        for j in range(4):
            for k in range(4):
                start = ((core + i) % 2) * 640 + ((y - j + 4) % 4) * 160 + ((x - k + 4) % 4) * 40
                packed_ref[pl.ds(pl.multiple_of(start, 8), 40), :] = part_ref[pl.ds(j * 160 + k * 40, 40), :]
    eye = lax.broadcasted_iota(jnp.int32, (128, 128), 0) == lax.broadcasted_iota(jnp.int32, (128, 128), 1)
    index = 0
    for i in range(4):
        for j in range(i + 1):
            block = packed_ref[pl.ds(index * 128, 128), :]
            if i == j:
                block = block + jnp.where(eye, RIDGE, 0.0)
            else:
                out_ref[pl.ds(j * 128, 128), pl.ds(i * 128, 128)] = block.T
            out_ref[pl.ds(i * 128, 128), pl.ds(j * 128, 128)] = block
            index += 1
    lane_block = lax.broadcasted_iota(jnp.int32, (512, 512), 1) // 128
    row_lane = lax.broadcasted_iota(jnp.int32, (128, 512), 1)
    row_sub = lax.broadcasted_iota(jnp.int32, (128, 512), 0)

    def stage(p, carry):
        start = pl.multiple_of(p * 128, 128)
        part = pl.ds(start, 128)
        column = out_ref[:, part]
        pivot = invert_block(out_ref[part, part])
        row = jnp.where(row_lane // 128 == p, (row_lane - start == row_sub).astype(jnp.float32), out_ref[part, :])
        scaled = jnp.dot(pivot, row, precision=HIGHEST, preferred_element_type=jnp.float32)
        rest = jnp.where(lane_block == p, 0.0, out_ref[...])
        out_ref[...] = rest - jnp.dot(column, scaled, precision=HIGHEST, preferred_element_type=jnp.float32)
        out_ref[part, :] = scaled
        return carry

    lax.fori_loop(0, 4, stage, 0)


def inverse(own, other):
    return pl.pallas_call(
        inverse_kernel,
        out_shape=jax.ShapeDtypeStruct((512, 512), jnp.float32),
        in_specs=[IN_VMEM] * 2,
        out_specs=IN_VMEM,
        scratch_shapes=[pltpu.VMEM((1280, 128), jnp.float32)],
        compiler_params=pltpu.CompilerParams(vmem_limit_bytes=32 * MIB),
        cost_estimate=pl.CostEstimate(flops=30000000000, bytes_accessed=2000000, transcendentals=0),
    )(own, other)


def align_kernel(rel_ref, block_ref, col_ref, flip_ref, values_ref, out_ref, place_ref, order_ref):
    def note(slot, carry):
        order_ref[col_ref[slot] // 2] = slot
        return carry

    lax.fori_loop(0, 64, note, 0)

    def move(step, carry):
        for i in range(8):
            index = step * 8 + i
            slot = jnp.where(index < 64, order_ref[jnp.minimum(index, 63)], index)
            flip = flip_ref[slot]
            place_ref[0, index] = col_ref[slot]
            place_ref[1, index] = flip * 8 + rel_ref[slot]
            place_ref[2, index] = block_ref[slot]
            tile = values_ref[slot]
            out_ref[index] = jnp.where(flip == 1, tile.T, tile)
        return carry

    lax.fori_loop(0, values_ref.shape[0] // 8, move, 0)


def align(tile_rel, tile_block, tile_col, tile_flip, values):
    slots = values.shape[0]
    return pl.pallas_call(
        align_kernel,
        out_shape=(
            jax.ShapeDtypeStruct(values.shape, values.dtype),
            jax.ShapeDtypeStruct((3, slots), jnp.int32),
        ),
        in_specs=[IN_SMEM] * 4 + [IN_VMEM],
        out_specs=(pl.BlockSpec(memory_space=pltpu.VMEM), IN_SMEM),
        scratch_shapes=[pltpu.SMEM((64,), jnp.int32)],
        compiler_params=pltpu.CompilerParams(vmem_limit_bytes=16 * MIB),
        cost_estimate=pl.CostEstimate(flops=3000000000, bytes_accessed=4800000, transcendentals=0),
    )(tile_rel, tile_block, tile_col, tile_flip, values)


def rows_kernel(
    count_ref, place_ref, values_ref, cores_ref, panels_ref, upper_ref, lower_ref, sums_ref, panel_ref, core_ref,
    sem, core_sem
):
    def fetch(owner):
        start = pl.multiple_of((place_ref[0, owner] % 2) * 128, 128)
        return pltpu.make_async_copy(panels_ref.at[owner, pl.ds(start, 128), :], panel_ref.at[owner], sem.at[owner])

    def begin(step, carry):
        for i in range(8):
            fetch(step * 8 + i).start()
        return carry

    lax.fori_loop(0, 8, begin, 0)
    core_copy = pltpu.make_async_copy(cores_ref, core_ref, core_sem)
    core_copy.start()
    sums_ref[...] = jnp.zeros_like(sums_ref)

    def add(index, owner):
        place = pl.multiple_of(place_ref[2, index] * 128, 128)
        term = product(values_ref[index], panel_ref[owner], 1, 0)
        where = (place_ref[1, index], pl.ds(place, 128), slice(None))
        sums_ref[where] = sums_ref[where] + term

    def main(step, carry):
        for i in range(8):
            fetch(step * 8 + i).wait()
        for i in range(8):
            add(step * 8 + i, step * 8 + i)
        return carry

    lax.fori_loop(0, 8, main, 0)

    def extra(index, carry):
        add(index, place_ref[0, index] // 2)
        return carry

    lax.fori_loop(64, count_ref[0], extra, 0)
    core_copy.wait()
    total = jnp.zeros((256, 512), jnp.float32)
    for k in range(8):
        core = core_ref[k]
        total += product(sums_ref[k].astype(jnp.bfloat16), core, 1, 1)
        total += product(sums_ref[k + 8].astype(jnp.bfloat16), core, 1, 0)
    rounded = total.astype(jnp.bfloat16)
    upper_ref[...] = rounded[:128]
    lower_ref[...] = rounded[128:]


def partial_rows(count, place, values, cores, panels):
    return pl.pallas_call(
        rows_kernel,
        out_shape=(jax.ShapeDtypeStruct((128, 512), jnp.bfloat16),) * 2,
        in_specs=[IN_SMEM, IN_SMEM, IN_VMEM] + [pl.BlockSpec(memory_space=pltpu.HBM)] * 2,
        out_specs=(IN_VMEM,) * 2,
        scratch_shapes=[
            pltpu.VMEM((16, 256, 512), jnp.float32),
            pltpu.VMEM((64, 128, 512), jnp.bfloat16),
            pltpu.VMEM(cores.shape, cores.dtype),
            pltpu.SemaphoreType.DMA((64,)),
            pltpu.SemaphoreType.DMA,
        ],
        compiler_params=pltpu.CompilerParams(vmem_limit_bytes=49 * MIB),
        cost_estimate=pl.CostEstimate(flops=10000000000, bytes_accessed=16000000, transcendentals=0),
    )(count, place, values, cores, panels)


def finish_kernel(upper_ref, upper_other_ref, lower_ref, lower_other_ref, inverse_ref, out_ref):
    wide = lambda ref: ref[...].astype(jnp.float32)
    upper = wide(upper_ref) + wide(upper_other_ref)
    lower = wide(lower_ref) + wide(lower_other_ref)
    rows = jnp.concatenate([upper, lower], axis=0)
    out_ref[...] = jnp.dot(rows, inverse_ref[...], precision=HIGHEST, preferred_element_type=jnp.float32)


def finish(upper, upper_other, lower, lower_other, inverted):
    return pl.pallas_call(
        finish_kernel,
        out_shape=jax.ShapeDtypeStruct((256, 512), jnp.float32),
        in_specs=[IN_VMEM] * 5,
        out_specs=IN_VMEM,
        compiler_params=pltpu.CompilerParams(vmem_limit_bytes=16 * MIB),
        cost_estimate=pl.CostEstimate(flops=1000000000, bytes_accessed=2500000, transcendentals=0),
    )(upper, upper_other, lower, lower_other, inverted)


def over_y(v, d):
    return lax.ppermute(v, "rel", [(y, (y + d) % 4) for y in range(4)])


def swap_y(v, bits):
    return lax.ppermute(v, "rel", [(y, y ^ bits) for y in range(4)])


def over_x(v, d):
    return lax.ppermute(v, "ent", [(e, (e + 16 * d) % 64) for e in range(64)])


def swap_z(v, bits):
    return lax.ppermute(v, "ent", [(e, e ^ (2 * bits)) for e in range(64)])


def swap_core(v):
    return lax.ppermute(v, "ent", [(e, e ^ 1) for e in range(64)])


def scatter_sum(part, send):
    quarter = part.shape[0] // 4
    arrived = [send(part[d * quarter:(d + 1) * quarter], d) for d in (1, 2, 3)]
    return (part[:quarter] + arrived[1]) + (arrived[0] + arrived[2])


def gather(part, send):
    return jnp.concatenate([part] + [send(part, d) for d in (1, 2, 3)], axis=0)


def sum_everywhere(placed):
    part = placed[:640] + swap_core(placed[640:])
    part = scatter_sum(part, over_y)
    part = scatter_sum(part, over_x)
    part = part + swap_z(part, 1)
    arrived = [swap_z(part, bits) for bits in (2, 4, 6)]
    part = (part + arrived[1]) + (arrived[0] + arrived[2])
    part = gather(gather(part, over_x), over_y)
    return part, swap_core(part)


def local(factor, core_tensors, tile_values, tile_rel, tile_block, tile_col, tile_flip, tile_count):
    panels = lax.all_gather(factor, "ent")
    inverted = inverse(*sum_everywhere(system_term(factor, core_tensors)))
    values, place = align(tile_rel[0], tile_block[0], tile_col[0], tile_flip[0], tile_values[0])
    panels, inverted, values, place = lax.optimization_barrier((panels, inverted, values, place))
    upper, lower = partial_rows(tile_count[0], place, values, core_tensors, panels)
    add = lambda a, b: (a.astype(jnp.float32) + b.astype(jnp.float32)).astype(jnp.bfloat16)
    upper, lower = add(upper, swap_y(upper, 1)), add(lower, swap_y(lower, 3))
    return finish(upper, swap_y(upper, 3), lower, swap_y(lower, 1), inverted)


def solution(mesh):
    in_specs = (
        P("ent", None),
        P("rel", None, None),
        P("rel", "ent", None, None),
        P("rel", "ent"),
        P("rel", "ent"),
        P("rel", "ent"),
        P("rel", "ent"),
        P("rel", "ent"),
    )
    out_specs = P("ent", None)
    return jax.shard_map(local, mesh=mesh, in_specs=in_specs, out_specs=out_specs, check_vma=False)
```

```python
import jax
import jax.numpy as jnp
from jax import lax
from jax.experimental import pallas as pl
from jax.experimental.pallas import tpu as pltpu
from jax.sharding import PartitionSpec as P

HIGHEST = lax.Precision.HIGHEST
MIB = 1024 * 1024
RIDGE = 16.0
IN_VMEM = pl.BlockSpec(memory_space=pltpu.VMEM)
IN_SMEM = pl.BlockSpec(memory_space=pltpu.SMEM)


def product(a, b, a_dim, b_dim):
    return lax.dot_general(a, b, (((a_dim,), (b_dim,)), ((), ())), preferred_element_type=jnp.float32)


def position():
    ent = lax.axis_index("ent")
    return ent // 16, lax.axis_index("rel"), ent % 2


def system_kernel(rows_ref, cores_ref, out_ref, core_ref, packed_ref, d0_ref, d1_ref, low_ref, c0_ref, c1_ref, sem):
    fetch = lambda step: pltpu.make_async_copy(cores_ref.at[step], core_ref.at[step], sem.at[step])
    for step in range(8):
        fetch(step).start()
    rows = rows_ref[...]
    for ref in (d0_ref, d1_ref, low_ref, c0_ref, c1_ref):
        ref[...] = jnp.zeros_like(ref)

    def body(step, carry):
        fetch(step).wait()
        core = core_ref[step]
        term = jnp.concatenate([product(rows, core, 1, 1), product(rows, core, 1, 0)], axis=0)
        high = term.astype(jnp.bfloat16)
        low = (term - high.astype(jnp.float32)).astype(jnp.bfloat16)
        h0, h1 = high[:, :256], high[:, 256:]
        l0, l1 = low[:, :256], low[:, 256:]
        h0t, h1t, l1t = h0.T, h1.T, l1.T
        d0_ref[...] += product(h0t, h0, 1, 0)
        d1_ref[...] += product(h1t, h1, 1, 0)
        c0_ref[...] += product(h0t, l0, 1, 0)
        c1_ref[...] += product(h1t, l1, 1, 0)
        low_ref[...] += product(h1t, h0, 1, 0) + product(h1t, l0, 1, 0) + product(l1t, h0, 1, 0)
        return carry

    lax.fori_loop(0, core_ref.shape[0], body, 0)
    first = d0_ref[...] + (c0_ref[...] + c0_ref[...].T)
    last = d1_ref[...] + (c1_ref[...] + c1_ref[...].T)
    mixed = low_ref[...]
    blocks = (
        first[:128, :128], first[128:, :128], first[128:, 128:],
        mixed[:128, :128], mixed[:128, 128:], last[:128, :128],
        mixed[128:, :128], mixed[128:, 128:], last[128:, :128], last[128:, 128:],
    )
    for index, block in enumerate(blocks):
        packed_ref[pl.ds(index * 128, 128), :] = block
    x, y, core = position()
    for c in range(2):
        for j in range(4):
            for k in range(4):
                start = ((c + core) % 2) * 640 + ((j - y + 4) % 4) * 160 + ((k - x + 4) % 4) * 40
                out_ref[pl.ds(pl.multiple_of(start, 8), 40), :] = packed_ref[pl.ds(c * 640 + j * 160 + k * 40, 40), :]


def system_term(factor, cores):
    return pl.pallas_call(
        system_kernel,
        out_shape=jax.ShapeDtypeStruct((1280, 128), jnp.float32),
        in_specs=[IN_VMEM, pl.BlockSpec(memory_space=pltpu.HBM)],
        out_specs=IN_VMEM,
        scratch_shapes=[pltpu.VMEM(cores.shape, cores.dtype), pltpu.VMEM((1280, 128), jnp.float32)]
        + [pltpu.VMEM((256, 256), jnp.float32)] * 5
        + [pltpu.SemaphoreType.DMA((8,))],
        compiler_params=pltpu.CompilerParams(vmem_limit_bytes=52 * MIB),
        cost_estimate=pl.CostEstimate(flops=12000000000, bytes_accessed=5000000, transcendentals=0),
    )(factor, cores)


def invert_block(m):
    full = (8, 128)
    blocks = [m[8 * r:8 * r + 8, :] for r in range(16)]
    lanes = lax.broadcasted_iota(jnp.int32, full, 1)
    subs = lax.broadcasted_iota(jnp.int32, full, 0)
    for q in range(16):
        panel = blocks[q]
        d = {
            (i, j): jnp.broadcast_to(panel[i:i + 1, 8 * q + j:8 * q + j + 1], full)
            for i in range(8)
            for j in range(i + 1)
        }
        entry = lambda i, j: d[max(i, j), min(i, j)]
        for k in range(8):
            inverse = 1.0 / d[k, k]
            ratio = {i: entry(i, k) * inverse for i in range(8) if i != k}
            for i in range(8):
                for j in range(i + 1):
                    if i != k and j != k:
                        d[i, j] = d[i, j] - ratio[i] * entry(j, k)
            for i in ratio:
                d[max(i, k), min(i, k)] = ratio[i]
            d[k, k] = -inverse
        inside = lanes // 8 == q
        unit = [
            jnp.broadcast_to(
                jnp.where(inside, (lanes == 8 * q + j).astype(jnp.float32), panel)[j:j + 1, :], full
            )
            for j in range(8)
        ]
        scaled = []
        for i in range(8):
            row = entry(i, 0) * unit[0]
            for j in range(1, 8):
                row = row + entry(i, j) * unit[j]
            scaled.append(row)
        for r in range(16):
            if r != q:
                old = blocks[r]
                new = jnp.where(inside, 0.0, old)
                for i in range(8):
                    new = new + jnp.broadcast_to(old[:, 8 * q + i:8 * q + i + 1], full) * scaled[i]
                blocks[r] = new
        row = scaled[0]
        for i in range(1, 8):
            row = jnp.where(subs == i, scaled[i], row)
        blocks[q] = -row
    return jnp.concatenate(blocks, axis=0)


def inverse_kernel(own_ref, other_ref, out_ref, packed_ref):
    x, y, core = position()
    for i, part_ref in enumerate((own_ref, other_ref)):
        for j in range(4):
            for k in range(4):
                start = ((core + i) % 2) * 640 + ((y - j + 4) % 4) * 160 + ((x - k + 4) % 4) * 40
                packed_ref[pl.ds(pl.multiple_of(start, 8), 40), :] = part_ref[pl.ds(j * 160 + k * 40, 40), :]
    eye = lax.broadcasted_iota(jnp.int32, (128, 128), 0) == lax.broadcasted_iota(jnp.int32, (128, 128), 1)
    index = 0
    for i in range(4):
        for j in range(i + 1):
            block = packed_ref[pl.ds(index * 128, 128), :]
            if i == j:
                block = block + jnp.where(eye, RIDGE, 0.0)
            else:
                out_ref[pl.ds(j * 128, 128), pl.ds(i * 128, 128)] = block.T
            out_ref[pl.ds(i * 128, 128), pl.ds(j * 128, 128)] = block
            index += 1
    lane_block = lax.broadcasted_iota(jnp.int32, (512, 512), 1) // 128
    row_lane = lax.broadcasted_iota(jnp.int32, (128, 512), 1)
    row_sub = lax.broadcasted_iota(jnp.int32, (128, 512), 0)

    def stage(p, carry):
        start = pl.multiple_of(p * 128, 128)
        part = pl.ds(start, 128)
        column = out_ref[:, part]
        pivot = invert_block(out_ref[part, part])
        row = jnp.where(row_lane // 128 == p, (row_lane - start == row_sub).astype(jnp.float32), out_ref[part, :])
        scaled = jnp.dot(pivot, row, precision=HIGHEST, preferred_element_type=jnp.float32)
        rest = jnp.where(lane_block == p, 0.0, out_ref[...])
        out_ref[...] = rest - jnp.dot(column, scaled, precision=HIGHEST, preferred_element_type=jnp.float32)
        out_ref[part, :] = scaled
        return carry

    lax.fori_loop(0, 4, stage, 0)


def inverse(own, other):
    return pl.pallas_call(
        inverse_kernel,
        out_shape=jax.ShapeDtypeStruct((512, 512), jnp.float32),
        in_specs=[IN_VMEM] * 2,
        out_specs=IN_VMEM,
        scratch_shapes=[pltpu.VMEM((1280, 128), jnp.float32)],
        compiler_params=pltpu.CompilerParams(vmem_limit_bytes=32 * MIB),
        cost_estimate=pl.CostEstimate(flops=30000000000, bytes_accessed=2000000, transcendentals=0),
    )(own, other)


def align_kernel(rel_ref, block_ref, col_ref, flip_ref, values_ref, out_ref, place_ref, order_ref):
    def note(slot, carry):
        order_ref[col_ref[slot] // 2] = slot
        return carry

    lax.fori_loop(0, 64, note, 0)

    def move(step, carry):
        for i in range(8):
            index = step * 8 + i
            slot = jnp.where(index < 64, order_ref[jnp.minimum(index, 63)], index)
            flip = flip_ref[slot]
            place_ref[0, index] = col_ref[slot]
            place_ref[1, index] = flip * 8 + rel_ref[slot]
            place_ref[2, index] = block_ref[slot]
            tile = values_ref[slot]
            out_ref[index] = jnp.where(flip == 1, tile.T, tile)
        return carry

    lax.fori_loop(0, values_ref.shape[0] // 8, move, 0)


def align(tile_rel, tile_block, tile_col, tile_flip, values):
    slots = values.shape[0]
    return pl.pallas_call(
        align_kernel,
        out_shape=(
            jax.ShapeDtypeStruct(values.shape, values.dtype),
            jax.ShapeDtypeStruct((3, slots), jnp.int32),
        ),
        in_specs=[IN_SMEM] * 4 + [IN_VMEM],
        out_specs=(pl.BlockSpec(memory_space=pltpu.VMEM), IN_SMEM),
        scratch_shapes=[pltpu.SMEM((64,), jnp.int32)],
        compiler_params=pltpu.CompilerParams(vmem_limit_bytes=16 * MIB),
        cost_estimate=pl.CostEstimate(flops=3000000000, bytes_accessed=4800000, transcendentals=0),
    )(tile_rel, tile_block, tile_col, tile_flip, values)


def rows_kernel(
    count_ref, place_ref, values_ref, cores_ref, panels_ref, own_ref, first_ref, second_ref, third_ref, sums_ref,
    panel_ref, core_ref, total_ref, sem, core_sem
):
    def fetch(owner):
        start = pl.multiple_of((place_ref[0, owner] % 2) * 128, 128)
        return pltpu.make_async_copy(panels_ref.at[owner, pl.ds(start, 128), :], panel_ref.at[owner], sem.at[owner])

    def begin(step, carry):
        for i in range(8):
            fetch(step * 8 + i).start()
        return carry

    lax.fori_loop(0, 8, begin, 0)
    core_copy = pltpu.make_async_copy(cores_ref, core_ref, core_sem)
    core_copy.start()
    sums_ref[...] = jnp.zeros_like(sums_ref)

    def add(index, owner):
        place = pl.multiple_of(place_ref[2, index] * 128, 128)
        term = product(values_ref[index], panel_ref[owner], 1, 0)
        where = (place_ref[1, index], pl.ds(place, 128), slice(None))
        sums_ref[where] = sums_ref[where] + term

    def main(step, carry):
        for i in range(8):
            fetch(step * 8 + i).wait()
        for i in range(8):
            add(step * 8 + i, step * 8 + i)
        return carry

    lax.fori_loop(0, 8, main, 0)

    def extra(index, carry):
        add(index, place_ref[0, index] // 2)
        return carry

    lax.fori_loop(64, count_ref[0], extra, 0)
    core_copy.wait()
    total = jnp.zeros((256, 512), jnp.float32)
    for k in range(8):
        core = core_ref[k]
        total += product(sums_ref[k].astype(jnp.bfloat16), core, 1, 1)
        total += product(sums_ref[k + 8].astype(jnp.bfloat16), core, 1, 0)
    total_ref[...] = total
    for d, ref in enumerate((own_ref, first_ref, second_ref, third_ref)):
        start = pl.multiple_of(((lax.axis_index("rel") + d) % 4) * 64, 64)
        ref[...] = total_ref[pl.ds(start, 64), :].astype(ref.dtype)


def partial_rows(count, place, values, cores, panels):
    return pl.pallas_call(
        rows_kernel,
        out_shape=(jax.ShapeDtypeStruct((64, 512), jnp.float32),)
        + (jax.ShapeDtypeStruct((64, 512), jnp.bfloat16),) * 3,
        in_specs=[IN_SMEM, IN_SMEM, IN_VMEM] + [pl.BlockSpec(memory_space=pltpu.HBM)] * 2,
        out_specs=(IN_VMEM,) * 4,
        scratch_shapes=[
            pltpu.VMEM((16, 256, 512), jnp.float32),
            pltpu.VMEM((64, 128, 512), jnp.bfloat16),
            pltpu.VMEM(cores.shape, cores.dtype),
            pltpu.VMEM((256, 512), jnp.float32),
            pltpu.SemaphoreType.DMA((64,)),
            pltpu.SemaphoreType.DMA,
        ],
        compiler_params=pltpu.CompilerParams(vmem_limit_bytes=49 * MIB),
        cost_estimate=pl.CostEstimate(flops=10000000000, bytes_accessed=16000000, transcendentals=0),
    )(count, place, values, cores, panels)


def finish_kernel(own_ref, first_ref, second_ref, third_ref, inverse_ref, out_ref):
    wide = lambda ref: ref[...].astype(jnp.float32)
    rows = (wide(own_ref) + wide(second_ref)) + (wide(first_ref) + wide(third_ref))
    solved = jnp.dot(rows, inverse_ref[...], precision=HIGHEST, preferred_element_type=jnp.float32)
    out_ref[...] = solved.astype(jnp.bfloat16)


def finish(own, arrived, inverted):
    return pl.pallas_call(
        finish_kernel,
        out_shape=jax.ShapeDtypeStruct(own.shape, jnp.bfloat16),
        in_specs=[IN_VMEM] * 5,
        out_specs=IN_VMEM,
        compiler_params=pltpu.CompilerParams(vmem_limit_bytes=16 * MIB),
        cost_estimate=pl.CostEstimate(flops=300000000, bytes_accessed=1500000, transcendentals=0),
    )(own, *arrived, inverted)


def assemble_kernel(own_ref, first_ref, second_ref, third_ref, out_ref):
    for d, ref in enumerate((own_ref, first_ref, second_ref, third_ref)):
        start = pl.multiple_of(((lax.axis_index("rel") - d + 4) % 4) * 64, 64)
        out_ref[pl.ds(start, 64), :] = ref[...].astype(jnp.float32)


def assemble(own, arrived):
    return pl.pallas_call(
        assemble_kernel,
        out_shape=jax.ShapeDtypeStruct((256, 512), jnp.float32),
        in_specs=[IN_VMEM] * 4,
        out_specs=IN_VMEM,
        compiler_params=pltpu.CompilerParams(vmem_limit_bytes=16 * MIB),
        cost_estimate=pl.CostEstimate(flops=100000, bytes_accessed=800000, transcendentals=0),
    )(own, *arrived)


def over_y(v, d):
    return lax.ppermute(v, "rel", [(y, (y + d) % 4) for y in range(4)])


def over_x(v, d):
    return lax.ppermute(v, "ent", [(e, (e + 16 * d) % 64) for e in range(64)])


def swap_z(v, bits):
    return lax.ppermute(v, "ent", [(e, e ^ (2 * bits)) for e in range(64)])


def swap_core(v):
    return lax.ppermute(v, "ent", [(e, e ^ 1) for e in range(64)])


def scatter_sum(part, send):
    quarter = part.shape[0] // 4
    arrived = [send(part[d * quarter:(d + 1) * quarter], d) for d in (1, 2, 3)]
    return (part[:quarter] + arrived[1]) + (arrived[0] + arrived[2])


def gather(part, send):
    return jnp.concatenate([part] + [send(part, d) for d in (1, 2, 3)], axis=0)


def sum_everywhere(placed):
    part = placed[:640] + swap_core(placed[640:])
    part = scatter_sum(part, over_y)
    part = scatter_sum(part, over_x)
    part = part + swap_z(part, 1)
    arrived = [swap_z(part, bits) for bits in (2, 4, 6)]
    part = (part + arrived[1]) + (arrived[0] + arrived[2])
    part = gather(gather(part, over_x), over_y)
    return part, swap_core(part)


def local(factor, core_tensors, tile_values, tile_rel, tile_block, tile_col, tile_flip, tile_count):
    panels = lax.all_gather(factor, "ent")
    inverted = inverse(*sum_everywhere(system_term(factor, core_tensors)))
    values, place = align(tile_rel[0], tile_block[0], tile_col[0], tile_flip[0], tile_values[0])
    panels, inverted, values, place = lax.optimization_barrier((panels, inverted, values, place))
    own, *others = partial_rows(tile_count[0], place, values, core_tensors, panels)
    own = finish(own, [over_y(other, d + 1) for d, other in enumerate(others)], inverted)
    return assemble(own, [over_y(own, d) for d in (1, 2, 3)])


def solution(mesh):
    in_specs = (
        P("ent", None),
        P("rel", None, None),
        P("rel", "ent", None, None),
        P("rel", "ent"),
        P("rel", "ent"),
        P("rel", "ent"),
        P("rel", "ent"),
        P("rel", "ent"),
    )
    out_specs = P("ent", None)
    return jax.shard_map(local, mesh=mesh, in_specs=in_specs, out_specs=out_specs, check_vma=False)
```

```python
import jax
import jax.numpy as jnp
from jax import lax
from jax.experimental import pallas as pl
from jax.experimental.pallas import tpu as pltpu
from jax.sharding import PartitionSpec as P

HIGHEST = lax.Precision.HIGHEST
MIB = 1024 * 1024
RIDGE = 16.0
IN_VMEM = pl.BlockSpec(memory_space=pltpu.VMEM)
IN_SMEM = pl.BlockSpec(memory_space=pltpu.SMEM)


def product(a, b, a_dim, b_dim):
    return lax.dot_general(a, b, (((a_dim,), (b_dim,)), ((), ())), preferred_element_type=jnp.float32)


def split(value):
    high = value.astype(jnp.bfloat16)
    return high, (value - high.astype(jnp.float32)).astype(jnp.bfloat16)


def position():
    ent = lax.axis_index("ent")
    return ent // 16, lax.axis_index("rel"), ent % 2


def system_kernel(rows_ref, cores_ref, out_ref, core_ref, packed_ref, d0_ref, d1_ref, low_ref, c0_ref, c1_ref, sem):
    fetch = lambda step: pltpu.make_async_copy(cores_ref.at[step], core_ref.at[step], sem.at[step])
    for step in range(8):
        fetch(step).start()
    rows = rows_ref[...]
    for ref in (d0_ref, d1_ref, low_ref, c0_ref, c1_ref):
        ref[...] = jnp.zeros_like(ref)

    def body(step, carry):
        fetch(step).wait()
        core = core_ref[step]
        term = jnp.concatenate([product(rows, core, 1, 1), product(rows, core, 1, 0)], axis=0)
        high = term.astype(jnp.bfloat16)
        low = (term - high.astype(jnp.float32)).astype(jnp.bfloat16)
        h0, h1 = high[:, :256], high[:, 256:]
        l0, l1 = low[:, :256], low[:, 256:]
        h0t, h1t, l1t = h0.T, h1.T, l1.T
        d0_ref[...] += product(h0t, h0, 1, 0)
        d1_ref[...] += product(h1t, h1, 1, 0)
        c0_ref[...] += product(h0t, l0, 1, 0)
        c1_ref[...] += product(h1t, l1, 1, 0)
        low_ref[...] += product(h1t, h0, 1, 0) + product(h1t, l0, 1, 0) + product(l1t, h0, 1, 0)
        return carry

    lax.fori_loop(0, core_ref.shape[0], body, 0)
    first = d0_ref[...] + (c0_ref[...] + c0_ref[...].T)
    last = d1_ref[...] + (c1_ref[...] + c1_ref[...].T)
    mixed = low_ref[...]
    blocks = (
        first[:128, :128], first[128:, :128], first[128:, 128:],
        mixed[:128, :128], mixed[:128, 128:], last[:128, :128],
        mixed[128:, :128], mixed[128:, 128:], last[128:, :128], last[128:, 128:],
    )
    for index, block in enumerate(blocks):
        packed_ref[pl.ds(index * 128, 128), :] = block
    x, y, core = position()
    for c in range(2):
        for j in range(4):
            for k in range(4):
                start = ((c + core) % 2) * 640 + ((j - y + 4) % 4) * 160 + ((k - x + 4) % 4) * 40
                out_ref[pl.ds(pl.multiple_of(start, 8), 40), :] = packed_ref[pl.ds(c * 640 + j * 160 + k * 40, 40), :]


def system_term(factor, cores):
    return pl.pallas_call(
        system_kernel,
        out_shape=jax.ShapeDtypeStruct((1280, 128), jnp.float32),
        in_specs=[IN_VMEM, pl.BlockSpec(memory_space=pltpu.HBM)],
        out_specs=IN_VMEM,
        scratch_shapes=[pltpu.VMEM(cores.shape, cores.dtype), pltpu.VMEM((1280, 128), jnp.float32)]
        + [pltpu.VMEM((256, 256), jnp.float32)] * 5
        + [pltpu.SemaphoreType.DMA((8,))],
        compiler_params=pltpu.CompilerParams(vmem_limit_bytes=52 * MIB),
        cost_estimate=pl.CostEstimate(flops=12000000000, bytes_accessed=5000000, transcendentals=0),
    )(factor, cores)


def invert_block(m):
    full = (8, 128)
    blocks = [m[8 * r:8 * r + 8, :] for r in range(16)]
    lanes = lax.broadcasted_iota(jnp.int32, full, 1)
    subs = lax.broadcasted_iota(jnp.int32, full, 0)
    for q in range(16):
        panel = blocks[q]
        d = {
            (i, j): jnp.broadcast_to(panel[i:i + 1, 8 * q + j:8 * q + j + 1], full)
            for i in range(8)
            for j in range(i + 1)
        }
        entry = lambda i, j: d[max(i, j), min(i, j)]
        for k in range(8):
            inverse = 1.0 / d[k, k]
            ratio = {i: entry(i, k) * inverse for i in range(8) if i != k}
            for i in range(8):
                for j in range(i + 1):
                    if i != k and j != k:
                        d[i, j] = d[i, j] - ratio[i] * entry(j, k)
            for i in ratio:
                d[max(i, k), min(i, k)] = ratio[i]
            d[k, k] = -inverse
        inside = lanes // 8 == q
        unit = [
            jnp.broadcast_to(
                jnp.where(inside, (lanes == 8 * q + j).astype(jnp.float32), panel)[j:j + 1, :], full
            )
            for j in range(8)
        ]
        scaled = []
        for i in range(8):
            row = entry(i, 0) * unit[0]
            for j in range(1, 8):
                row = row + entry(i, j) * unit[j]
            scaled.append(row)
        for r in range(16):
            if r != q:
                old = blocks[r]
                new = jnp.where(inside, 0.0, old)
                for i in range(8):
                    new = new + jnp.broadcast_to(old[:, 8 * q + i:8 * q + i + 1], full) * scaled[i]
                blocks[r] = new
        row = scaled[0]
        for i in range(1, 8):
            row = jnp.where(subs == i, scaled[i], row)
        blocks[q] = -row
    return jnp.concatenate(blocks, axis=0)


def inverse_kernel(own_ref, other_ref, out_ref, packed_ref):
    x, y, core = position()
    for i, part_ref in enumerate((own_ref, other_ref)):
        for j in range(4):
            for k in range(4):
                start = ((core + i) % 2) * 640 + ((y - j + 4) % 4) * 160 + ((x - k + 4) % 4) * 40
                packed_ref[pl.ds(pl.multiple_of(start, 8), 40), :] = part_ref[pl.ds(j * 160 + k * 40, 40), :]
    eye = lax.broadcasted_iota(jnp.int32, (128, 128), 0) == lax.broadcasted_iota(jnp.int32, (128, 128), 1)
    index = 0
    for i in range(4):
        for j in range(i + 1):
            block = packed_ref[pl.ds(index * 128, 128), :]
            if i == j:
                block = block + jnp.where(eye, RIDGE, 0.0)
            else:
                out_ref[pl.ds(j * 128, 128), pl.ds(i * 128, 128)] = block.T
            out_ref[pl.ds(i * 128, 128), pl.ds(j * 128, 128)] = block
            index += 1
    lane_block = lax.broadcasted_iota(jnp.int32, (512, 512), 1) // 128
    row_lane = lax.broadcasted_iota(jnp.int32, (128, 512), 1)
    row_sub = lax.broadcasted_iota(jnp.int32, (128, 512), 0)

    def stage(p, carry):
        start = pl.multiple_of(p * 128, 128)
        part = pl.ds(start, 128)
        column = out_ref[:, part]
        pivot = invert_block(out_ref[part, part])
        row = jnp.where(row_lane // 128 == p, (row_lane - start == row_sub).astype(jnp.float32), out_ref[part, :])
        scaled = jnp.dot(pivot, row, precision=HIGHEST, preferred_element_type=jnp.float32)
        rest = jnp.where(lane_block == p, 0.0, out_ref[...])
        out_ref[...] = rest - jnp.dot(column, scaled, precision=HIGHEST, preferred_element_type=jnp.float32)
        out_ref[part, :] = scaled
        return carry

    lax.fori_loop(0, 4, stage, 0)


def inverse(own, other):
    return pl.pallas_call(
        inverse_kernel,
        out_shape=jax.ShapeDtypeStruct((512, 512), jnp.float32),
        in_specs=[IN_VMEM] * 2,
        out_specs=IN_VMEM,
        scratch_shapes=[pltpu.VMEM((1280, 128), jnp.float32)],
        compiler_params=pltpu.CompilerParams(vmem_limit_bytes=32 * MIB),
        cost_estimate=pl.CostEstimate(flops=30000000000, bytes_accessed=2000000, transcendentals=0),
    )(own, other)


def align_kernel(rel_ref, block_ref, col_ref, flip_ref, values_ref, out_ref, place_ref, order_ref):
    def note(slot, carry):
        order_ref[col_ref[slot] // 2] = slot
        return carry

    lax.fori_loop(0, 64, note, 0)

    def move(step, carry):
        for i in range(8):
            index = step * 8 + i
            slot = jnp.where(index < 64, order_ref[jnp.minimum(index, 63)], index)
            flip = flip_ref[slot]
            place_ref[0, index] = col_ref[slot]
            place_ref[1, index] = flip * 8 + rel_ref[slot]
            place_ref[2, index] = block_ref[slot]
            tile = values_ref[slot]
            out_ref[index] = jnp.where(flip == 1, tile.T, tile)
        return carry

    lax.fori_loop(0, values_ref.shape[0] // 8, move, 0)


def align(tile_rel, tile_block, tile_col, tile_flip, values):
    slots = values.shape[0]
    return pl.pallas_call(
        align_kernel,
        out_shape=(
            jax.ShapeDtypeStruct(values.shape, values.dtype),
            jax.ShapeDtypeStruct((3, slots), jnp.int32),
        ),
        in_specs=[IN_SMEM] * 4 + [IN_VMEM],
        out_specs=(pl.BlockSpec(memory_space=pltpu.VMEM), IN_SMEM),
        scratch_shapes=[pltpu.SMEM((64,), jnp.int32)],
        compiler_params=pltpu.CompilerParams(vmem_limit_bytes=16 * MIB),
        cost_estimate=pl.CostEstimate(flops=3000000000, bytes_accessed=4800000, transcendentals=0),
    )(tile_rel, tile_block, tile_col, tile_flip, values)


def rows_kernel(
    count_ref, place_ref, values_ref, cores_ref, panels_ref, upper_ref, lower_ref, sums_ref, panel_ref, core_ref,
    sem, core_sem
):
    def fetch(owner):
        start = pl.multiple_of((place_ref[0, owner] % 2) * 128, 128)
        return pltpu.make_async_copy(panels_ref.at[owner, pl.ds(start, 128), :], panel_ref.at[owner], sem.at[owner])

    def begin(step, carry):
        for i in range(8):
            fetch(step * 8 + i).start()
        return carry

    lax.fori_loop(0, 8, begin, 0)
    core_copy = pltpu.make_async_copy(cores_ref, core_ref, core_sem)
    core_copy.start()
    sums_ref[...] = jnp.zeros_like(sums_ref)

    def add(index, owner):
        place = pl.multiple_of(place_ref[2, index] * 128, 128)
        term = product(values_ref[index], panel_ref[owner], 1, 0)
        where = (place_ref[1, index], pl.ds(place, 128), slice(None))
        sums_ref[where] = sums_ref[where] + term

    def main(step, carry):
        for i in range(16):
            fetch(step * 16 + i).wait()
        for i in range(16):
            add(step * 16 + i, step * 16 + i)
        return carry

    lax.fori_loop(0, 4, main, 0)

    def extra(index, carry):
        add(index, place_ref[0, index] // 2)
        return carry

    lax.fori_loop(64, count_ref[0], extra, 0)
    core_copy.wait()
    total = jnp.zeros((256, 512), jnp.float32)
    for k in range(8):
        core = core_ref[k]
        total += product(sums_ref[k].astype(jnp.bfloat16), core, 1, 1)
        total += product(sums_ref[k + 8].astype(jnp.bfloat16), core, 1, 0)
    rounded = total.astype(jnp.bfloat16)
    upper_ref[...] = rounded[:128]
    lower_ref[...] = rounded[128:]


def partial_rows(count, place, values, cores, panels):
    return pl.pallas_call(
        rows_kernel,
        out_shape=(jax.ShapeDtypeStruct((128, 512), jnp.bfloat16),) * 2,
        in_specs=[IN_SMEM, IN_SMEM, IN_VMEM] + [pl.BlockSpec(memory_space=pltpu.HBM)] * 2,
        out_specs=(IN_VMEM,) * 2,
        scratch_shapes=[
            pltpu.VMEM((16, 256, 512), jnp.float32),
            pltpu.VMEM((64, 128, 512), jnp.bfloat16),
            pltpu.VMEM(cores.shape, cores.dtype),
            pltpu.SemaphoreType.DMA((64,)),
            pltpu.SemaphoreType.DMA,
        ],
        compiler_params=pltpu.CompilerParams(vmem_limit_bytes=49 * MIB),
        cost_estimate=pl.CostEstimate(flops=10000000000, bytes_accessed=16000000, transcendentals=0),
    )(count, place, values, cores, panels)


def finish_kernel(upper_ref, upper_other_ref, lower_ref, lower_other_ref, inverse_ref, out_ref):
    wide = lambda ref: ref[...].astype(jnp.float32)
    upper = wide(upper_ref) + wide(upper_other_ref)
    lower = wide(lower_ref) + wide(lower_other_ref)
    rows = jnp.concatenate([upper, lower], axis=0)
    high, low = split(rows)
    inverse_high, inverse_low = split(inverse_ref[...])
    small = product(low, inverse_high, 1, 0) + product(high, inverse_low, 1, 0)
    out_ref[...] = product(high, inverse_high, 1, 0) + small


def finish(upper, upper_other, lower, lower_other, inverted):
    return pl.pallas_call(
        finish_kernel,
        out_shape=jax.ShapeDtypeStruct((256, 512), jnp.float32),
        in_specs=[IN_VMEM] * 5,
        out_specs=IN_VMEM,
        compiler_params=pltpu.CompilerParams(vmem_limit_bytes=16 * MIB),
        cost_estimate=pl.CostEstimate(flops=1000000000, bytes_accessed=2500000, transcendentals=0),
    )(upper, upper_other, lower, lower_other, inverted)


def over_y(v, d):
    return lax.ppermute(v, "rel", [(y, (y + d) % 4) for y in range(4)])


def swap_y(v, bits):
    return lax.ppermute(v, "rel", [(y, y ^ bits) for y in range(4)])


def over_x(v, d):
    return lax.ppermute(v, "ent", [(e, (e + 16 * d) % 64) for e in range(64)])


def swap_z(v, bits):
    return lax.ppermute(v, "ent", [(e, e ^ (2 * bits)) for e in range(64)])


def swap_core(v):
    return lax.ppermute(v, "ent", [(e, e ^ 1) for e in range(64)])


def scatter_sum(part, send):
    quarter = part.shape[0] // 4
    arrived = [send(part[d * quarter:(d + 1) * quarter], d) for d in (1, 2, 3)]
    return (part[:quarter] + arrived[1]) + (arrived[0] + arrived[2])


def gather(part, send):
    return jnp.concatenate([part] + [send(part, d) for d in (1, 2, 3)], axis=0)


def sum_everywhere(placed):
    part = placed[:640] + swap_core(placed[640:])
    part = scatter_sum(part, over_y)
    part = scatter_sum(part, over_x)
    part = part + swap_z(part, 1)
    arrived = [swap_z(part, bits) for bits in (2, 4, 6)]
    part = (part + arrived[1]) + (arrived[0] + arrived[2])
    part = gather(gather(part, over_x), over_y)
    return part, swap_core(part)


def local(factor, core_tensors, tile_values, tile_rel, tile_block, tile_col, tile_flip, tile_count):
    panels = lax.all_gather(factor, "ent")
    inverted = inverse(*sum_everywhere(system_term(factor, core_tensors)))
    values, place = align(tile_rel[0], tile_block[0], tile_col[0], tile_flip[0], tile_values[0])
    panels, inverted, values, place = lax.optimization_barrier((panels, inverted, values, place))
    upper, lower = partial_rows(tile_count[0], place, values, core_tensors, panels)
    add = lambda a, b: (a.astype(jnp.float32) + b.astype(jnp.float32)).astype(jnp.bfloat16)
    upper, lower = add(upper, swap_y(upper, 1)), add(lower, swap_y(lower, 3))
    return finish(upper, swap_y(upper, 3), lower, swap_y(lower, 1), inverted)


def solution(mesh):
    in_specs = (
        P("ent", None),
        P("rel", None, None),
        P("rel", "ent", None, None),
        P("rel", "ent"),
        P("rel", "ent"),
        P("rel", "ent"),
        P("rel", "ent"),
        P("rel", "ent"),
    )
    out_specs = P("ent", None)
    return jax.shard_map(local, mesh=mesh, in_specs=in_specs, out_specs=out_specs, check_vma=False)
```

```python
import jax
import jax.numpy as jnp
from jax import lax
from jax.experimental import pallas as pl
from jax.experimental.pallas import tpu as pltpu
from jax.sharding import PartitionSpec as P

HIGHEST = lax.Precision.HIGHEST
MIB = 1024 * 1024
RIDGE = 16.0
IN_VMEM = pl.BlockSpec(memory_space=pltpu.VMEM)
IN_SMEM = pl.BlockSpec(memory_space=pltpu.SMEM)


def product(a, b, a_dim, b_dim):
    return lax.dot_general(a, b, (((a_dim,), (b_dim,)), ((), ())), preferred_element_type=jnp.float32)


def split(value):
    high = value.astype(jnp.bfloat16)
    return high, (value - high.astype(jnp.float32)).astype(jnp.bfloat16)


def position():
    ent = lax.axis_index("ent")
    return ent // 16, lax.axis_index("rel"), ent % 2


def system_kernel(rows_ref, cores_ref, out_ref, core_ref, packed_ref, d0_ref, d1_ref, low_ref, c0_ref, c1_ref, sem):
    fetch = lambda step: pltpu.make_async_copy(cores_ref.at[step], core_ref.at[step], sem.at[step])
    for step in range(8):
        fetch(step).start()
    rows = rows_ref[...]
    for ref in (d0_ref, d1_ref, low_ref, c0_ref, c1_ref):
        ref[...] = jnp.zeros_like(ref)

    def body(step, carry):
        fetch(step).wait()
        core = core_ref[step]
        term = jnp.concatenate([product(rows, core, 1, 1), product(rows, core, 1, 0)], axis=0)
        high = term.astype(jnp.bfloat16)
        low = (term - high.astype(jnp.float32)).astype(jnp.bfloat16)
        h0, h1 = high[:, :256], high[:, 256:]
        l0, l1 = low[:, :256], low[:, 256:]
        h0t, h1t, l1t = h0.T, h1.T, l1.T
        d0_ref[...] += product(h0t, h0, 1, 0)
        d1_ref[...] += product(h1t, h1, 1, 0)
        c0_ref[...] += product(h0t, l0, 1, 0)
        c1_ref[...] += product(h1t, l1, 1, 0)
        low_ref[...] += product(h1t, h0, 1, 0) + product(h1t, l0, 1, 0) + product(l1t, h0, 1, 0)
        return carry

    lax.fori_loop(0, core_ref.shape[0], body, 0)
    first = d0_ref[...] + (c0_ref[...] + c0_ref[...].T)
    last = d1_ref[...] + (c1_ref[...] + c1_ref[...].T)
    mixed = low_ref[...]
    blocks = (
        first[:128, :128], first[128:, :128], first[128:, 128:],
        mixed[:128, :128], mixed[:128, 128:], last[:128, :128],
        mixed[128:, :128], mixed[128:, 128:], last[128:, :128], last[128:, 128:],
    )
    for index, block in enumerate(blocks):
        packed_ref[pl.ds(index * 128, 128), :] = block
    x, y, core = position()
    for c in range(2):
        for j in range(4):
            for k in range(4):
                start = ((c + core) % 2) * 640 + ((j - y + 4) % 4) * 160 + ((k - x + 4) % 4) * 40
                out_ref[pl.ds(pl.multiple_of(start, 8), 40), :] = packed_ref[pl.ds(c * 640 + j * 160 + k * 40, 40), :]


def system_term(factor, cores):
    return pl.pallas_call(
        system_kernel,
        out_shape=jax.ShapeDtypeStruct((1280, 128), jnp.float32),
        in_specs=[IN_VMEM, pl.BlockSpec(memory_space=pltpu.HBM)],
        out_specs=IN_VMEM,
        scratch_shapes=[pltpu.VMEM(cores.shape, cores.dtype), pltpu.VMEM((1280, 128), jnp.float32)]
        + [pltpu.VMEM((256, 256), jnp.float32)] * 5
        + [pltpu.SemaphoreType.DMA((8,))],
        compiler_params=pltpu.CompilerParams(vmem_limit_bytes=52 * MIB),
        cost_estimate=pl.CostEstimate(flops=12000000000, bytes_accessed=5000000, transcendentals=0),
    )(factor, cores)


def invert_block(m):
    full = (8, 128)
    blocks = [m[8 * r:8 * r + 8, :] for r in range(16)]
    lanes = lax.broadcasted_iota(jnp.int32, full, 1)
    subs = lax.broadcasted_iota(jnp.int32, full, 0)
    for q in range(16):
        panel = blocks[q]
        d = {
            (i, j): jnp.broadcast_to(panel[i:i + 1, 8 * q + j:8 * q + j + 1], full)
            for i in range(8)
            for j in range(i + 1)
        }
        entry = lambda i, j: d[max(i, j), min(i, j)]
        for k in range(8):
            inverse = 1.0 / d[k, k]
            ratio = {i: entry(i, k) * inverse for i in range(8) if i != k}
            for i in range(8):
                for j in range(i + 1):
                    if i != k and j != k:
                        d[i, j] = d[i, j] - ratio[i] * entry(j, k)
            for i in ratio:
                d[max(i, k), min(i, k)] = ratio[i]
            d[k, k] = -inverse
        inside = lanes // 8 == q
        unit = [
            jnp.broadcast_to(
                jnp.where(inside, (lanes == 8 * q + j).astype(jnp.float32), panel)[j:j + 1, :], full
            )
            for j in range(8)
        ]
        scaled = []
        for i in range(8):
            row = entry(i, 0) * unit[0]
            for j in range(1, 8):
                row = row + entry(i, j) * unit[j]
            scaled.append(row)
        for r in range(16):
            if r != q:
                old = blocks[r]
                new = jnp.where(inside, 0.0, old)
                for i in range(8):
                    new = new + jnp.broadcast_to(old[:, 8 * q + i:8 * q + i + 1], full) * scaled[i]
                blocks[r] = new
        row = scaled[0]
        for i in range(1, 8):
            row = jnp.where(subs == i, scaled[i], row)
        blocks[q] = -row
    return jnp.concatenate(blocks, axis=0)


def inverse_kernel(own_ref, other_ref, out_ref, packed_ref):
    x, y, core = position()
    for i, part_ref in enumerate((own_ref, other_ref)):
        for j in range(4):
            for k in range(4):
                start = ((core + i) % 2) * 640 + ((y - j + 4) % 4) * 160 + ((x - k + 4) % 4) * 40
                packed_ref[pl.ds(pl.multiple_of(start, 8), 40), :] = part_ref[pl.ds(j * 160 + k * 40, 40), :]
    eye = lax.broadcasted_iota(jnp.int32, (128, 128), 0) == lax.broadcasted_iota(jnp.int32, (128, 128), 1)
    index = 0
    for i in range(4):
        for j in range(i + 1):
            block = packed_ref[pl.ds(index * 128, 128), :]
            if i == j:
                block = block + jnp.where(eye, RIDGE, 0.0)
            else:
                out_ref[pl.ds(j * 128, 128), pl.ds(i * 128, 128)] = block.T
            out_ref[pl.ds(i * 128, 128), pl.ds(j * 128, 128)] = block
            index += 1
    lane_block = lax.broadcasted_iota(jnp.int32, (512, 512), 1) // 128
    row_lane = lax.broadcasted_iota(jnp.int32, (128, 512), 1)
    row_sub = lax.broadcasted_iota(jnp.int32, (128, 512), 0)

    def stage(p, carry):
        start = pl.multiple_of(p * 128, 128)
        part = pl.ds(start, 128)
        column = out_ref[:, part]
        pivot = invert_block(out_ref[part, part])
        row = jnp.where(row_lane // 128 == p, (row_lane - start == row_sub).astype(jnp.float32), out_ref[part, :])
        scaled = jnp.dot(pivot, row, precision=HIGHEST, preferred_element_type=jnp.float32)
        rest = jnp.where(lane_block == p, 0.0, out_ref[...])
        out_ref[...] = rest - jnp.dot(column, scaled, precision=HIGHEST, preferred_element_type=jnp.float32)
        out_ref[part, :] = scaled
        return carry

    lax.fori_loop(0, 4, stage, 0)


def inverse(own, other):
    return pl.pallas_call(
        inverse_kernel,
        out_shape=jax.ShapeDtypeStruct((512, 512), jnp.float32),
        in_specs=[IN_VMEM] * 2,
        out_specs=IN_VMEM,
        scratch_shapes=[pltpu.VMEM((1280, 128), jnp.float32)],
        compiler_params=pltpu.CompilerParams(vmem_limit_bytes=32 * MIB),
        cost_estimate=pl.CostEstimate(flops=30000000000, bytes_accessed=2000000, transcendentals=0),
    )(own, other)


def align_kernel(rel_ref, block_ref, col_ref, flip_ref, values_ref, out_ref, place_ref, order_ref):
    def note(slot, carry):
        order_ref[col_ref[slot] // 2] = slot
        return carry

    lax.fori_loop(0, 64, note, 0)

    def move(step, carry):
        for i in range(8):
            index = step * 8 + i
            slot = jnp.where(index < 64, order_ref[jnp.minimum(index, 63)], index)
            flip = flip_ref[slot]
            place_ref[0, index] = col_ref[slot]
            place_ref[1, index] = flip * 8 + rel_ref[slot]
            place_ref[2, index] = block_ref[slot]
            tile = values_ref[slot]
            out_ref[index] = jnp.where(flip == 1, tile.T, tile)
        return carry

    lax.fori_loop(0, values_ref.shape[0] // 8, move, 0)


def align(tile_rel, tile_block, tile_col, tile_flip, values):
    slots = values.shape[0]
    return pl.pallas_call(
        align_kernel,
        out_shape=(
            jax.ShapeDtypeStruct(values.shape, values.dtype),
            jax.ShapeDtypeStruct((3, slots), jnp.int32),
        ),
        in_specs=[IN_SMEM] * 4 + [IN_VMEM],
        out_specs=(pl.BlockSpec(memory_space=pltpu.VMEM), IN_SMEM),
        scratch_shapes=[pltpu.SMEM((64,), jnp.int32)],
        compiler_params=pltpu.CompilerParams(vmem_limit_bytes=16 * MIB),
        cost_estimate=pl.CostEstimate(flops=3000000000, bytes_accessed=4800000, transcendentals=0),
    )(tile_rel, tile_block, tile_col, tile_flip, values)


def rows_kernel(
    count_ref, place_ref, values_ref, cores_ref, panels_ref, upper_ref, lower_ref, sums_ref, panel_ref, core_ref,
    sem, core_sem
):
    def fetch(owner):
        start = pl.multiple_of((place_ref[0, owner] % 2) * 128, 128)
        return pltpu.make_async_copy(panels_ref.at[owner, pl.ds(start, 128), :], panel_ref.at[owner], sem.at[owner])

    def begin(step, carry):
        for i in range(8):
            fetch(step * 8 + i).start()
        return carry

    lax.fori_loop(0, 8, begin, 0)
    core_copy = pltpu.make_async_copy(cores_ref, core_ref, core_sem)
    core_copy.start()
    sums_ref[...] = jnp.zeros_like(sums_ref)

    def add(index, owner):
        place = pl.multiple_of(place_ref[2, index] * 128, 128)
        term = product(values_ref[index], panel_ref[owner], 1, 0)
        where = (place_ref[1, index], pl.ds(place, 128), slice(None))
        sums_ref[where] = sums_ref[where] + term

    def main(step, carry):
        for i in range(16):
            fetch(step * 16 + i).wait()
        for i in range(16):
            add(step * 16 + i, step * 16 + i)
        return carry

    lax.fori_loop(0, 4, main, 0, unroll=True)

    def extra(index, carry):
        add(index, place_ref[0, index] // 2)
        return carry

    lax.fori_loop(64, count_ref[0], extra, 0)
    core_copy.wait()
    total = jnp.zeros((256, 512), jnp.float32)
    for k in range(8):
        core = core_ref[k]
        total += product(sums_ref[k].astype(jnp.bfloat16), core, 1, 1)
        total += product(sums_ref[k + 8].astype(jnp.bfloat16), core, 1, 0)
    rounded = total.astype(jnp.bfloat16)
    upper_ref[...] = rounded[:128]
    lower_ref[...] = rounded[128:]


def partial_rows(count, place, values, cores, panels):
    return pl.pallas_call(
        rows_kernel,
        out_shape=(jax.ShapeDtypeStruct((128, 512), jnp.bfloat16),) * 2,
        in_specs=[IN_SMEM, IN_SMEM, IN_VMEM] + [pl.BlockSpec(memory_space=pltpu.HBM)] * 2,
        out_specs=(IN_VMEM,) * 2,
        scratch_shapes=[
            pltpu.VMEM((16, 256, 512), jnp.float32),
            pltpu.VMEM((64, 128, 512), jnp.bfloat16),
            pltpu.VMEM(cores.shape, cores.dtype),
            pltpu.SemaphoreType.DMA((64,)),
            pltpu.SemaphoreType.DMA,
        ],
        compiler_params=pltpu.CompilerParams(vmem_limit_bytes=49 * MIB),
        cost_estimate=pl.CostEstimate(flops=10000000000, bytes_accessed=16000000, transcendentals=0),
    )(count, place, values, cores, panels)


def finish_kernel(upper_ref, upper_other_ref, lower_ref, lower_other_ref, inverse_ref, out_ref):
    wide = lambda ref: ref[...].astype(jnp.float32)
    upper = wide(upper_ref) + wide(upper_other_ref)
    lower = wide(lower_ref) + wide(lower_other_ref)
    rows = jnp.concatenate([upper, lower], axis=0)
    high, low = split(rows)
    inverse_high, inverse_low = split(inverse_ref[...])
    small = product(low, inverse_high, 1, 0) + product(high, inverse_low, 1, 0)
    out_ref[...] = product(high, inverse_high, 1, 0) + small


def finish(upper, upper_other, lower, lower_other, inverted):
    return pl.pallas_call(
        finish_kernel,
        out_shape=jax.ShapeDtypeStruct((256, 512), jnp.float32),
        in_specs=[IN_VMEM] * 5,
        out_specs=IN_VMEM,
        compiler_params=pltpu.CompilerParams(vmem_limit_bytes=16 * MIB),
        cost_estimate=pl.CostEstimate(flops=1000000000, bytes_accessed=2500000, transcendentals=0),
    )(upper, upper_other, lower, lower_other, inverted)


def over_y(v, d):
    return lax.ppermute(v, "rel", [(y, (y + d) % 4) for y in range(4)])


def swap_y(v, bits):
    return lax.ppermute(v, "rel", [(y, y ^ bits) for y in range(4)])


def over_x(v, d):
    return lax.ppermute(v, "ent", [(e, (e + 16 * d) % 64) for e in range(64)])


def swap_z(v, bits):
    return lax.ppermute(v, "ent", [(e, e ^ (2 * bits)) for e in range(64)])


def swap_core(v):
    return lax.ppermute(v, "ent", [(e, e ^ 1) for e in range(64)])


def scatter_sum(part, send):
    quarter = part.shape[0] // 4
    arrived = [send(part[d * quarter:(d + 1) * quarter], d) for d in (1, 2, 3)]
    return (part[:quarter] + arrived[1]) + (arrived[0] + arrived[2])


def gather(part, send):
    return jnp.concatenate([part] + [send(part, d) for d in (1, 2, 3)], axis=0)


def sum_everywhere(placed):
    part = placed[:640] + swap_core(placed[640:])
    part = scatter_sum(part, over_y)
    part = scatter_sum(part, over_x)
    part = part + swap_z(part, 1)
    arrived = [swap_z(part, bits) for bits in (2, 4, 6)]
    part = (part + arrived[1]) + (arrived[0] + arrived[2])
    part = gather(gather(part, over_x), over_y)
    return part, swap_core(part)


def local(factor, core_tensors, tile_values, tile_rel, tile_block, tile_col, tile_flip, tile_count):
    panels = lax.all_gather(factor, "ent")
    inverted = inverse(*sum_everywhere(system_term(factor, core_tensors)))
    values, place = align(tile_rel[0], tile_block[0], tile_col[0], tile_flip[0], tile_values[0])
    panels, inverted, values, place = lax.optimization_barrier((panels, inverted, values, place))
    upper, lower = partial_rows(tile_count[0], place, values, core_tensors, panels)
    add = lambda a, b: (a.astype(jnp.float32) + b.astype(jnp.float32)).astype(jnp.bfloat16)
    upper, lower = add(upper, swap_y(upper, 1)), add(lower, swap_y(lower, 3))
    return finish(upper, swap_y(upper, 3), lower, swap_y(lower, 1), inverted)


def solution(mesh):
    in_specs = (
        P("ent", None),
        P("rel", None, None),
        P("rel", "ent", None, None),
        P("rel", "ent"),
        P("rel", "ent"),
        P("rel", "ent"),
        P("rel", "ent"),
        P("rel", "ent"),
    )
    out_specs = P("ent", None)
    return jax.shard_map(local, mesh=mesh, in_specs=in_specs, out_specs=out_specs, check_vma=False)
```
